256 devices in a mesh: dp: 16 (over z, y_lo), seq: 16 (over y_hi, x, core).
Axes of the slice: x: 4, y: 4 (y_hi: 2, y_lo: 2; y = y_hi * 2 + y_lo), z: 8, core: 2. Of those that a mesh axis runs over, the one named last changes fastest.
Arguments:
- trunk_acts: bfloat16 [16, 16384, 768], P('dp', 'seq'), may hold values from -6 to 6
- base_ids: int32 [16, 16384], P('dp', 'seq'), may hold values from 0 to 3
- base_table: float32 [4, 768], replicated, may hold values from -6 to 6
- norm_gain: float32 [768], replicated, may hold values from 0.1 to 1.9
- conv_weight: bfloat16 [768, 3, 768], replicated, may hold values from -0.125 to 0.125
- grad_out: bfloat16 [16, 16384, 768], P('dp', 'seq'), may hold values from -6 to 6
- donor_pos: int32 [16, 32768], P('dp', 'seq'), may hold values from 0 to 1023
- accept_pos: int32 [16, 32768], P('dp', 'seq'), may hold values from 0 to 1023
- pair_counts: int32 [16, 256], P('dp', 'seq'), may hold values from 1 to 128, as said below
- donor_weight: bfloat16 [768, 768], replicated, may hold values from -0.21875 to 0.21875
- accept_weight: bfloat16 [768, 768], replicated, may hold values from -0.21875 to 0.21875
Outputs:
- junction_pairs: bfloat16 [16, 32768, 768], P('dp', 'seq')
- weight_grad: float32 [768, 3, 768], P('seq', None, 'dp')
The draws below stay inside these ranges and needn't reach their ends.
Inputs may be any that keep to these rules, and one draw needn't show every extreme that they name: `pair_counts`: for every interval one acceptor owner has all 128 slots valid from every sender; the other counts lie from 1 to 64.
All inputs are finite; a program needn't handle non-finite values.
Results may differ from the reference program's by a relative error of at most 0.0067.
Values may be sent and summed in bfloat16 or wider, within the bound.
No kernel may reach another device: no remote copies, remote signals or barrier semaphores. Data moves between devices by JAX's collectives and lax.ppermute only.
A program may use at most 128 MiB of HBM per device.

```python
import jax
import jax.numpy as jnp
from jax import lax

C = 768
KERNEL_TAPS = 3
DILATION_STEP = 256
L_DEV = 1024
CAP = 128
INTERVALS = 16
INTERVAL_LENGTH = 16384
JROWS = 32768
N_SEQ = 16


def draw_pair_counts(key, part):
    key_fill, key_hot = jax.random.split(jax.random.fold_in(key, 17))
    random_fill = jax.random.randint(key_fill, (INTERVALS, N_SEQ, N_SEQ), 1, CAP // 2 + 1)
    hot_owner = jax.random.randint(key_hot, (INTERVALS, 1, 1), 0, N_SEQ)
    owner_ids = jnp.arange(N_SEQ).astype(jnp.int32)[None, None, :]
    filled = jnp.where(owner_ids == hot_owner, CAP, random_fill)
    return filled.reshape(INTERVALS, N_SEQ * N_SEQ).astype(jnp.int32)


def set_ends(entries, rng, low, top_value):
    place = [jax.random.randint(jax.random.fold_in(rng, axis), (), 0, length) for axis, length in enumerate(entries.shape)]
    longest = entries.shape.index(max(entries.shape))
    neighbour = place[:longest] + [(place[longest] + 1) % entries.shape[longest]] + place[longest + 1:]
    return entries.at[tuple(place)].set(low).at[tuple(neighbour)].set(top_value)


def spiked(drawn, key, source, target, shards_of, factor):
    def block_of(axis_at):
        return (jnp.arange(drawn.shape[axis_at]) // (drawn.shape[axis_at] // shards_of)).reshape((-1,) + (1,) * (drawn.ndim - 1 - axis_at))

    near = jax.random.permutation(key, shards_of)[block_of(target)]
    other_side = (block_of(target) + shards_of // 2) % shards_of
    return jnp.where((block_of(source) == near) | (block_of(source) == other_side), factor * drawn, drawn)


def steps_of(rng, extent, cuts, smallest, largest):
    gain, own = 1.0, jax.random.fold_in(rng, 6)
    for position, shards_of in cuts:
        steps = jnp.exp(jax.random.uniform(jax.random.fold_in(own, position), (shards_of,), jnp.float32, smallest / len(cuts), largest / len(cuts)))
        gain = gain * jnp.repeat(steps, extent[position] // shards_of).reshape([-1 if axis == position else 1 for axis in range(len(extent))])
    return gain


def gaussian(stream_key, dims, deviation, bound, shards=(), held_as=jnp.bfloat16):
    loudness = steps_of(stream_key, dims, shards, -0.22, 0.18) if shards else 1.0
    drawn = jax.random.normal(stream_key, dims, jnp.float32) * deviation * loudness
    return jnp.minimum(jnp.maximum(drawn, -bound), bound).astype(held_as)


def heavy_noise(key, shape, width, bound, shards, heavy, dtype=jnp.bfloat16):
    entries = width * jax.random.normal(key, shape, jnp.float32)
    if shards:
        entries = entries * steps_of(key, shape, shards, -0.22, 0.18)
    return jnp.clip(spiked(entries, jax.random.fold_in(key, 3), *heavy), -bound, bound).astype(dtype)


def setup_inputs(seed: int = 0) -> dict:
    seeds = jax.random.split(jax.random.key(seed), 12)
    return {
        "trunk_acts": heavy_noise(seeds[0], (INTERVALS, INTERVAL_LENGTH, C), 1.0, 6.0, ((0, 16), (1, 16)), (1, 2, 16, 2.0)),
        "base_ids": set_ends(jax.random.randint(seeds[1], (INTERVALS, INTERVAL_LENGTH), 0, 4), jax.random.fold_in(seeds[1], 1), 0, 3).astype(jnp.int32),
        "base_table": gaussian(seeds[2], (4, C), 1.0, 6.0, (), jnp.float32),
        "norm_gain": jnp.clip(1.0 + 0.18 * jax.random.normal(seeds[3], (C,), jnp.float32), 0.1, 1.9),
        "conv_weight": gaussian(seeds[4], (C, KERNEL_TAPS, C), (KERNEL_TAPS * C) ** -0.5, 0.125),
        "grad_out": heavy_noise(seeds[5], (INTERVALS, INTERVAL_LENGTH, C), 1.0, 6.0, ((0, 16), (1, 16)), (0, 2, 16, 2.0)),
        "donor_pos": set_ends(jax.random.randint(seeds[6], (INTERVALS, JROWS), 0, L_DEV), jax.random.fold_in(seeds[6], 1), 0, L_DEV - 1).astype(jnp.int32),
        "accept_pos": set_ends(jax.random.randint(seeds[7], (INTERVALS, JROWS), 0, L_DEV), jax.random.fold_in(seeds[7], 1), 0, L_DEV - 1).astype(jnp.int32),
        "pair_counts": draw_pair_counts(jax.random.fold_in(seeds[11], 71), 0),
        "donor_weight": gaussian(seeds[9], (C, C), C ** -0.5, 0.21875),
        "accept_weight": gaussian(seeds[10], (C, C), C ** -0.5, 0.21875),
    }


def rms_normed(inputs, norm_gain):
    scale = lax.rsqrt(lax.optimization_barrier(jnp.mean(inputs * inputs, axis=-1, keepdims=True)) + 1e-06)
    return (inputs * scale * norm_gain).astype(jnp.bfloat16)

def reference(trunk_acts, base_ids, base_table, norm_gain, conv_weight, grad_out, donor_pos, accept_pos, pair_counts, donor_weight, accept_weight):
    receptive_reach = DILATION_STEP * (KERNEL_TAPS // 2)
    row_ids = jnp.arange(JROWS).astype(jnp.int32)
    sender = row_ids // (N_SEQ * CAP)
    owner = row_ids // CAP % N_SEQ
    slot_ids = row_ids % CAP

    def one_interval(grad_total, packed):
        trunk, id_row, grad_row, donors, accepts, counts = packed
        onehot = (id_row[:, None] == jnp.arange(4).astype(jnp.int32)[None, :]).astype(jnp.float32)
        inputs = trunk.astype(jnp.float32) + jnp.dot(onehot, base_table, precision=lax.Precision.HIGHEST)
        normalized_rows = rms_normed(inputs, norm_gain)
        padded_input = jnp.pad(normalized_rows, ((receptive_reach, receptive_reach), (0, 0)))
        sliding_windows = [padded_input[kernel_tap * DILATION_STEP:kernel_tap * DILATION_STEP + INTERVAL_LENGTH] for kernel_tap in range(KERNEL_TAPS)]
        conv_out = jnp.zeros((INTERVAL_LENGTH, C), jnp.float32)
        for kernel_tap in range(KERNEL_TAPS):
            conv_out = conv_out + jnp.dot(sliding_windows[kernel_tap], conv_weight[:, kernel_tap, :], preferred_element_type=jnp.float32)
        hidden = (inputs + jax.nn.gelu(conv_out)).astype(jnp.bfloat16)
        _, pull_back = jax.vjp(jax.nn.gelu, conv_out)
        dconv = pull_back(grad_row.astype(jnp.float32))[0].astype(jnp.bfloat16)
        terms = jnp.stack([lax.dot_general(win, dconv, (((0,), (0,)), ((), ())), preferred_element_type=jnp.float32) for win in sliding_windows], axis=1)
        accept_all = jnp.dot(hidden, accept_weight, preferred_element_type=jnp.float32).astype(jnp.bfloat16)
        donor_all = jnp.dot(hidden, donor_weight, preferred_element_type=jnp.float32)
        donor_index = (sender * L_DEV + donors).astype(jnp.int32)
        accept_index = (owner * L_DEV + accepts).astype(jnp.int32)
        valid = slot_ids < counts[(sender * N_SEQ + owner).astype(jnp.int32)]
        pairs = jnp.where(valid[:, None], donor_all[donor_index] * accept_all[accept_index].astype(jnp.float32), 0.0).astype(jnp.bfloat16)
        return (grad_total + terms, pairs)
    start_grad = jnp.zeros((C, KERNEL_TAPS, C), jnp.float32)
    weight_grad, junction_pairs = lax.scan(one_interval, start_grad, (trunk_acts, base_ids, grad_out, donor_pos, accept_pos, pair_counts))
    return (junction_pairs, weight_grad)
```

```python
import jax
import jax.numpy as jnp
from jax import lax
from jax.sharding import Mesh, PartitionSpec as P

DILATION_STEP = 256
AXES = ("z", "yl", "yh", "x", "core")
DP = ("z", "yl")
SEQ = ("yh", "x", "core")


def halos(block, width):
    count = lax.axis_size(SEQ)
    forward = [(i, i + 1) for i in range(count - 1)]
    backward = [(target, source) for source, target in forward]
    low = lax.ppermute(block[block.shape[0] - width :], SEQ, forward)
    high = lax.ppermute(block[:width], SEQ, backward)
    return low, high


def rms_normed(inputs, norm_gain):
    scale = lax.rsqrt(jnp.mean(inputs * inputs, axis=-1, keepdims=True) + 1e-06)
    return (inputs * scale * norm_gain).astype(jnp.bfloat16)


def picked_rows(table, index):
    onehot = (index[:, None] == jnp.arange(table.shape[0])[None, :]).astype(table.dtype)
    return jnp.dot(onehot, table, preferred_element_type=jnp.float32).astype(table.dtype)


def reduced_grad(windows, dconv):
    width = dconv.shape[1]
    core = lax.axis_index("core")
    seq_count = lax.axis_size(SEQ)
    dp_count = lax.axis_size(DP)
    chips = seq_count // 2
    rows, cols = width // seq_count, width // dp_count
    taps = len(windows)
    grad = jnp.stack(
        [
            lax.dot_general(win, dconv, (((0,), (0,)), ((), ())), preferred_element_type=jnp.float32)
            for win in windows
        ],
        axis=0,
    ).reshape(taps, chips, 2, rows, width)
    sent = lax.dynamic_index_in_dim(grad, 1 - core, 2, keepdims=False).astype(jnp.bfloat16)
    kept = lax.dynamic_index_in_dim(grad, core, 2, keepdims=False)
    other = lax.ppermute(sent, "core", [(0, 1), (1, 0)])
    chip_sum = (kept + other.astype(jnp.float32)).astype(jnp.bfloat16)
    pieces = jnp.transpose(chip_sum, (1, 0, 2, 3)).reshape(chips, taps * rows, width)
    pieces = lax.all_to_all(pieces, ("yh", "x"), 0, 0, tiled=True)
    own = jnp.sum(pieces.astype(jnp.float32), axis=0).astype(jnp.bfloat16)
    turned = own.T.reshape(dp_count, cols, taps * rows)
    turned = lax.all_to_all(turned, DP, 0, 0, tiled=True)
    total = jnp.sum(turned.astype(jnp.float32), axis=0)
    return jnp.transpose(total.reshape(cols, taps, rows), (2, 1, 0))


def on_device(
    trunk_acts,
    base_ids,
    base_table,
    norm_gain,
    conv_weight,
    grad_out,
    donor_pos,
    accept_pos,
    pair_counts,
    donor_weight,
    accept_weight,
):
    seq_count = lax.axis_size(SEQ)
    trunk = trunk_acts[0]
    length, width = trunk.shape
    slot_block = lax.all_to_all(accept_pos[0].reshape(seq_count, -1), SEQ, 0, 0, tiled=True)
    ids = base_ids[0][:, None]
    embedded = jnp.where(
        ids < 2,
        jnp.where(ids == 0, base_table[0:1], base_table[1:2]),
        jnp.where(ids == 2, base_table[2:3], base_table[3:4]),
    )
    inputs = trunk.astype(jnp.float32) + embedded
    rows = rms_normed(inputs, norm_gain)
    low, high = halos(rows, DILATION_STEP)
    windows = [
        jnp.concatenate([low, rows[: length - DILATION_STEP]], axis=0),
        rows,
        jnp.concatenate([rows[DILATION_STEP:], high], axis=0),
    ]
    conv_out = jnp.zeros((length, width), jnp.float32)
    for tap in (1, 0, 2):
        conv_out = conv_out + jnp.dot(
            windows[tap], conv_weight[:, tap, :], preferred_element_type=jnp.float32
        )
    hidden = (inputs + jax.nn.gelu(conv_out)).astype(jnp.bfloat16)
    _, pull_back = jax.vjp(jax.nn.gelu, conv_out)
    dconv = pull_back(grad_out[0].astype(jnp.float32))[0].astype(jnp.bfloat16)

    accept_local = jnp.dot(hidden, accept_weight, preferred_element_type=jnp.float32).astype(
        jnp.bfloat16
    )
    picked = picked_rows(accept_local, slot_block.reshape(-1)).reshape(seq_count, -1, width)
    accepted = lax.all_to_all(picked, SEQ, 0, 0, tiled=True).reshape(-1, width)

    weight_grad = reduced_grad(windows, dconv)

    donor_emb = jnp.dot(
        picked_rows(hidden, donor_pos[0]), donor_weight, preferred_element_type=jnp.float32
    )
    slots = donor_pos.shape[1] // seq_count
    valid = (jnp.arange(slots)[None, :] < pair_counts[0][:, None]).reshape(-1)
    junction_pairs = jnp.where(
        valid[:, None], donor_emb * accepted.astype(jnp.float32), 0.0
    ).astype(jnp.bfloat16)[None]
    return (junction_pairs, weight_grad)


def solution(mesh):
    grid = Mesh(mesh.devices.reshape(8, 2, 2, 4, 2), AXES)
    return jax.shard_map(
        on_device,
        mesh=grid,
        in_specs=(
            P(DP, SEQ, None),
            P(DP, SEQ),
            P(),
            P(),
            P(),
            P(DP, SEQ, None),
            P(DP, SEQ),
            P(DP, SEQ),
            P(DP, SEQ),
            P(),
            P(),
        ),
        out_specs=(P(DP, SEQ, None), P(SEQ, None, DP)),
        check_vma=False,
    )
```

```python
import functools

import jax
import jax.numpy as jnp
from jax import lax
from jax.experimental import pallas as pl
from jax.experimental.pallas import tpu as pltpu
from jax.sharding import Mesh, PartitionSpec as P

DILATION_STEP = 256
AXES = ("z", "yl", "yh", "x", "core")
DP = ("z", "yl")
SEQ = ("yh", "x", "core")
CHIPS = ("yh", "x")
LANES = 128
VMEM_BYTES = 48 * 1024 * 1024
BF16 = jnp.bfloat16
F32 = jnp.float32
GELU_A = 0.7978845608028654
GELU_B = 0.044715


def params():
    return pltpu.CompilerParams(vmem_limit_bytes=VMEM_BYTES)


def cost(flops, nbytes):
    return pl.CostEstimate(flops=flops, bytes_accessed=nbytes, transcendentals=0)


def across_lanes(row):
    return jnp.transpose(jnp.broadcast_to(row, (LANES, LANES)))


def summed_inputs(trunk, ids_ref, first, table_ref):
    rows, width = trunk.shape
    parts = []
    for block in range(rows // LANES):
        ids = across_lanes(ids_ref[pl.ds(first + block, 1), :])
        ids = jnp.concatenate([ids] * (width // LANES), axis=1)
        embedded = jnp.where(
            ids < 2,
            jnp.where(ids == 0, table_ref[0:1, :], table_ref[1:2, :]),
            jnp.where(ids == 2, table_ref[2:3, :], table_ref[3:4, :]),
        )
        parts.append(trunk[block * LANES : (block + 1) * LANES].astype(F32) + embedded)
    return jnp.concatenate(parts, axis=0)


def norm_kernel(trunk_ref, ids_ref, table_ref, gain_ref, out_ref):
    per_chunk = trunk_ref.shape[0] // LANES
    inputs = summed_inputs(trunk_ref[...], ids_ref, pl.program_id(0) * per_chunk, table_ref)
    mean = jnp.mean(inputs * inputs, axis=-1, keepdims=True)
    out_ref[...] = (inputs * lax.rsqrt(mean + 1e-06) * gain_ref[...]).astype(BF16)


def norm_rows(trunk, ids, table, gain):
    length, width = trunk.shape
    chunk = DILATION_STEP
    whole = lambda i: (0, 0)
    return pl.pallas_call(
        norm_kernel,
        grid=(length // chunk,),
        in_specs=[
            pl.BlockSpec((chunk, width), lambda i: (i, 0)),
            pl.BlockSpec(ids.shape, whole),
            pl.BlockSpec(table.shape, whole),
            pl.BlockSpec(gain.shape, whole),
        ],
        out_specs=pl.BlockSpec((chunk, width), lambda i: (i, 0)),
        out_shape=jax.ShapeDtypeStruct((length, width), BF16),
        compiler_params=params(),
        cost_estimate=cost(10 * length * width, 4 * length * width),
    )(trunk, ids, table, gain)


def gelu_parts(x):
    square = x * x
    t = jnp.tanh(GELU_A * x * (1.0 + GELU_B * square))
    cdf = 0.5 + 0.5 * t
    slope = cdf + (0.5 * GELU_A) * x * (1.0 - t * t) * (1.0 + (3 * GELU_B) * square)
    return x * cdf, slope


def finish_chunk(conv, trunk, grad, ids_ref, first, table_ref, hidden_ref, dconv_ref):
    inputs = summed_inputs(trunk, ids_ref, first, table_ref)
    act, slope = gelu_parts(conv)
    hidden_ref[...] = (inputs + act).astype(BF16)
    dconv_ref[...] = (grad.astype(F32) * slope).astype(BF16)


def turned(block, rows):
    width = block.shape[1]
    return jnp.transpose(block).reshape(width // (2 * rows), 2, rows, block.shape[0])


def inner_kernel(left_ref, mid_ref, right_ref, w_ref, trunk_ref, grad_ref, ids_ref, table_ref, all_ref,
                 hidden_ref, dconv_ref, turned_ref, *, rows):
    i = pl.program_id(0)
    window = jnp.concatenate([left_ref[...], mid_ref[...], right_ref[...]], axis=1)
    conv = jnp.dot(window, w_ref[...], preferred_element_type=F32)
    finish_chunk(conv, trunk_ref[...], grad_ref[...], ids_ref, 2 * (i + 1), table_ref, hidden_ref, dconv_ref)
    chunk = left_ref.shape[0]
    turned_ref[:, :, :, :chunk] = turned(all_ref[:chunk], rows)
    turned_ref[:, :, :, chunk:] = turned(all_ref[chunk:], rows)


def edge_kernel(low_ref, high_ref, near_ref, mid_ref, w_ref, trunk_ref, grad_ref, ids_ref, table_ref, h_in, d_in,
                hidden_ref, dconv_ref, low_t_ref, high_t_ref, acc_ref, *, rows):
    del h_in, d_in
    i = pl.program_id(0)
    width = mid_ref.shape[1]

    @pl.when(i == 0)
    def _():
        window = jnp.concatenate([low_ref[...], mid_ref[...], near_ref[...]], axis=1)
        acc_ref[...] = jnp.dot(window, w_ref[...], preferred_element_type=F32)
        low_t_ref[...] = turned(low_ref[...], rows)

    @pl.when(i == 1)
    def _():
        window = jnp.concatenate([near_ref[...], mid_ref[...], high_ref[...]], axis=1)
        acc_ref[...] = jnp.dot(window, w_ref[...], preferred_element_type=F32)
        high_t_ref[...] = turned(high_ref[...], rows)

    finish_chunk(acc_ref[...], trunk_ref[...], grad_ref[...], ids_ref, 6 * i, table_ref, hidden_ref, dconv_ref)


def conv_inner(normed, weight, trunk, grad, ids, table, rows):
    length, width = trunk.shape
    chunk = DILATION_STEP
    whole = lambda i: (0, 0)
    block = lambda shift: pl.BlockSpec((chunk, width), lambda i: (i + shift, 0))
    groups = width // (2 * rows)
    return pl.pallas_call(
        functools.partial(inner_kernel, rows=rows),
        grid=(2,),
        in_specs=[
            block(0), block(1), block(2),
            pl.BlockSpec(weight.shape, whole),
            block(1), block(1),
            pl.BlockSpec(ids.shape, whole),
            pl.BlockSpec(table.shape, whole),
            pl.BlockSpec((2 * chunk, width), lambda i: (i, 0)),
        ],
        out_specs=[
            block(1), block(1),
            pl.BlockSpec((groups, 2, rows, 2 * chunk), lambda i: (0, 0, 0, i)),
        ],
        out_shape=[
            jax.ShapeDtypeStruct((length, width), BF16),
            jax.ShapeDtypeStruct((length, width), BF16),
            jax.ShapeDtypeStruct((groups, 2, rows, length), BF16),
        ],
        compiler_params=params(),
        cost_estimate=cost(3 * length * width * width, 8 * length * width),
    )(normed, normed, normed, weight, trunk, grad, ids, table, normed)


def conv_edges(low, high, normed, weight, trunk, grad, ids, table, hidden, dconv, rows):
    length, width = trunk.shape
    chunk = DILATION_STEP
    whole = lambda i: (0, 0)
    outer = pl.BlockSpec((chunk, width), lambda i: (3 * i, 0))
    groups = width // (2 * rows)
    t_spec = pl.BlockSpec((groups, 2, rows, chunk), lambda i: (0, 0, 0, 0))
    t_shape = jax.ShapeDtypeStruct((groups, 2, rows, chunk), BF16)
    return pl.pallas_call(
        functools.partial(edge_kernel, rows=rows),
        grid=(2,),
        in_specs=[
            pl.BlockSpec(low.shape, whole),
            pl.BlockSpec(high.shape, whole),
            pl.BlockSpec((chunk, width), lambda i: (i + 1, 0)),
            outer,
            pl.BlockSpec(weight.shape, whole),
            outer, outer,
            pl.BlockSpec(ids.shape, whole),
            pl.BlockSpec(table.shape, whole),
            pl.BlockSpec(memory_space=pl.ANY),
            pl.BlockSpec(memory_space=pl.ANY),
        ],
        out_specs=[outer, outer, t_spec, t_spec],
        out_shape=[
            jax.ShapeDtypeStruct((length, width), BF16),
            jax.ShapeDtypeStruct((length, width), BF16),
            t_shape, t_shape,
        ],
        scratch_shapes=[pltpu.VMEM((chunk, width), F32)],
        input_output_aliases={9: 0, 10: 1},
        compiler_params=params(),
        cost_estimate=cost(3 * length * width * width, 8 * length * width),
    )(low, high, normed, normed, weight, trunk, grad, ids, table, hidden, dconv)


def grad_kernel(half_ref, turned_ref, low_ref, high_ref, dconv_ref, *rest, add):
    del half_ref
    other_ref, out_ref = rest if add else (None, rest[0])
    groups, _, rows, length = turned_ref.shape
    edge = low_ref.shape[3]
    tap = pl.program_id(0)
    flat = lambda v: v.reshape(groups * rows, v.shape[-1])
    dot = lambda a, b: jnp.dot(a, b, preferred_element_type=F32)

    def put(value):
        if add:
            value = value + flat(other_ref[:, 0]).astype(F32)
        out_ref[:, 0] = value.reshape(groups, rows, value.shape[-1]).astype(BF16)

    @pl.when(tap == 0)
    def _():
        window = jnp.concatenate([flat(low_ref[:, 0]), flat(turned_ref[:, 0, :, : length - edge])], axis=1)
        put(dot(window, dconv_ref[...]))

    @pl.when(tap == 1)
    def _():
        put(dot(flat(turned_ref[:, 0]), dconv_ref[...]))

    @pl.when(tap == 2)
    def _():
        window = jnp.concatenate([flat(turned_ref[:, 0, :, edge:]), flat(high_ref[:, 0])], axis=1)
        put(dot(window, dconv_ref[...]))


def grad_half(half, turned_rows, low_t, high_t, dconv, other=None):
    groups, _, rows, length = turned_rows.shape
    width = dconv.shape[1]
    taps = 3
    pick = lambda t, h: (0, h[0], 0, 0)
    out_spec = pl.BlockSpec((groups, 1, rows, width), lambda t, h: (0, t, 0, 0))
    specs = [
        pl.BlockSpec((groups, 1, rows, length), pick),
        pl.BlockSpec((groups, 1, rows, low_t.shape[3]), pick),
        pl.BlockSpec((groups, 1, rows, high_t.shape[3]), pick),
        pl.BlockSpec(dconv.shape, lambda t, h: (0, 0)),
    ]
    args = [half, turned_rows, low_t, high_t, dconv]
    if other is not None:
        specs.append(out_spec)
        args.append(other)
    return pl.pallas_call(
        functools.partial(grad_kernel, add=other is not None),
        grid_spec=pltpu.PrefetchScalarGridSpec(
            num_scalar_prefetch=1, grid=(taps,), in_specs=specs, out_specs=out_spec
        ),
        out_shape=jax.ShapeDtypeStruct((groups, taps, rows, width), BF16),
        compiler_params=params(),
        cost_estimate=cost(taps * length * width * width, 6 * length * width),
    )(*args)


def selected(index_row, table_ref):
    index = across_lanes(index_row)
    lane = lax.broadcasted_iota(jnp.int32, (LANES, LANES), 1)
    blocks = [
        jnp.where(index == lane + b * LANES, 1.0, 0.0).astype(BF16)
        for b in range(table_ref.shape[0] // LANES)
    ]
    return jnp.dot(jnp.concatenate(blocks, axis=1), table_ref[...], preferred_element_type=F32)


def serve_kernel(hot_ref, place_ref, index_ref, own_ref, other_ref, out_ref):
    del place_ref
    half = LANES // 2
    own = selected(index_ref[0, 0:1, :], own_ref).astype(BF16)
    other = selected(index_ref[0, 1:2, :], other_ref).astype(BF16)
    out_ref[0, 0] = own[:half]
    out_ref[0, 1] = other[:half]

    @pl.when(hot_ref[0] == 0)
    def _():
        out_ref[0, 2] = own[half:]

    @pl.when(hot_ref[0] != 0)
    def _():
        out_ref[0, 2] = other[half:]


def serve(hot, place, index, own, other):
    groups = index.shape[0]
    width = own.shape[1]
    whole = lambda q, h, p: (0, 0)
    return pl.pallas_call(
        serve_kernel,
        grid_spec=pltpu.PrefetchScalarGridSpec(
            num_scalar_prefetch=2,
            grid=(groups,),
            in_specs=[
                pl.BlockSpec((1, 2, LANES), lambda q, h, p: (p[q], 0, 0)),
                pl.BlockSpec(own.shape, whole),
                pl.BlockSpec(other.shape, whole),
            ],
            out_specs=pl.BlockSpec((1, 3, LANES // 2, width), lambda q, h, p: (q, 0, 0, 0)),
        ),
        out_shape=jax.ShapeDtypeStruct((groups, 3, LANES // 2, width), BF16),
        compiler_params=params(),
        cost_estimate=cost(4 * groups * LANES * own.shape[0] * width, 8 * own.size),
    )(hot, place, index, own, other)


def donor_kernel(index_ref, hidden_ref, w_ref, out_ref):
    for b in range(2):
        rows = selected(index_ref[0, b : b + 1, :], hidden_ref).astype(BF16)
        out_ref[b * LANES : (b + 1) * LANES] = jnp.dot(rows, w_ref[...], preferred_element_type=F32)


def donor_rows(index, hidden, weight):
    groups = index.shape[0]
    width = hidden.shape[1]
    whole = lambda q: (0, 0)
    return pl.pallas_call(
        donor_kernel,
        grid=(groups,),
        in_specs=[
            pl.BlockSpec((1, 2, LANES), lambda q: (q, 0, 0)),
            pl.BlockSpec(hidden.shape, whole),
            pl.BlockSpec(weight.shape, whole),
        ],
        out_specs=pl.BlockSpec((2 * LANES, width), lambda q: (q, 0)),
        out_shape=jax.ShapeDtypeStruct((groups * 2 * LANES, width), F32),
        compiler_params=params(),
        cost_estimate=cost(4 * groups * LANES * (hidden.shape[0] + width) * width, 10 * hidden.size),
    )(index, hidden, weight)


def pair_kernel(core_ref, counts_ref, donor_ref, accepted_ref, out_ref):
    half = LANES // 2
    group = pl.program_id(0)
    slot = lax.broadcasted_iota(jnp.int32, (half, out_ref.shape[1]), 0)
    for owner_core in range(2):
        count = counts_ref[2 * group + owner_core]
        place = lax.rem(core_ref[0] + owner_core, 2)
        first = owner_core * LANES
        lower = accepted_ref[0, place].astype(F32) * donor_ref[first : first + half]
        out_ref[first : first + half] = jnp.where(slot < count, lower, 0.0).astype(BF16)
        upper = accepted_ref[0, 2].astype(F32) * donor_ref[first + half : first + LANES]
        out_ref[first + half : first + LANES] = jnp.where(slot + half < count, upper, 0.0).astype(BF16)


def pairs(core, counts, donor, accepted):
    groups = accepted.shape[0]
    width = donor.shape[1]
    return pl.pallas_call(
        pair_kernel,
        grid_spec=pltpu.PrefetchScalarGridSpec(
            num_scalar_prefetch=2,
            grid=(groups,),
            in_specs=[
                pl.BlockSpec((2 * LANES, width), lambda q, c, n: (q, 0)),
                pl.BlockSpec((1,) + accepted.shape[1:], lambda q, c, n: (q, 0, 0, 0)),
            ],
            out_specs=pl.BlockSpec((2 * LANES, width), lambda q, c, n: (q, 0)),
        ),
        out_shape=jax.ShapeDtypeStruct(donor.shape, BF16),
        compiler_params=params(),
        cost_estimate=cost(2 * donor.size, 8 * donor.size),
    )(core, counts, donor, accepted)


def halos(block, width):
    count = lax.axis_size(SEQ)
    forward = [(i, i + 1) for i in range(count - 1)]
    backward = [(target, source) for source, target in forward]
    low = lax.ppermute(block[block.shape[0] - width :], SEQ, forward)
    high = lax.ppermute(block[:width], SEQ, backward)
    return low, high


def chip_exchange(blocks):
    ny, nx = lax.axis_size("yh"), lax.axis_size("x")
    y, x = lax.axis_index("yh"), lax.axis_index("x")
    got = []
    for step in range(ny * nx):
        dy, dx = step // nx, step % nx
        target = lax.rem(y + dy, ny) * nx + lax.rem(x + dx, nx)
        block = lax.dynamic_index_in_dim(blocks, target, 0, keepdims=False)
        if step:
            perm = [
                (i * nx + j, (i + dy) % ny * nx + (j + dx) % nx) for i in range(ny) for j in range(nx)
            ]
            block = lax.ppermute(block, CHIPS, perm)
        got.append(block)
    sources = jnp.arange(ny * nx)
    steps = lax.rem(y - sources // nx + ny, ny) * nx + lax.rem(x - sources % nx + nx, nx)
    return jnp.stack(got), steps


def dp_sum(own):
    nz = lax.axis_size("z")
    z, yl = lax.axis_index("z"), lax.axis_index("yl")
    blocks = own.reshape(nz, -1, own.shape[1])
    narrow = blocks.astype(BF16)
    total = lax.dynamic_index_in_dim(blocks, z, 0, keepdims=False)
    for step in range(1, nz):
        sent = lax.dynamic_index_in_dim(narrow, lax.rem(z + step, nz), 0, keepdims=False)
        got = lax.ppermute(sent, "z", [(i, (i + step) % nz) for i in range(nz)])
        total = total + got.astype(F32)
    total = total.reshape(2, -1, own.shape[1])
    sent = lax.dynamic_index_in_dim(total, 1 - yl, 0, keepdims=False).astype(BF16)
    kept = lax.dynamic_index_in_dim(total, yl, 0, keepdims=False)
    return kept + lax.ppermute(sent, "yl", [(0, 1), (1, 0)]).astype(F32)


def on_device(
    trunk_acts,
    base_ids,
    base_table,
    norm_gain,
    conv_weight,
    grad_out,
    donor_pos,
    accept_pos,
    pair_counts,
    donor_weight,
    accept_weight,
):
    seq_count = lax.axis_size(SEQ)
    core = lax.axis_index("core")
    chip = lax.axis_index(CHIPS)
    trunk, grad = trunk_acts[0], grad_out[0]
    length, width = trunk.shape
    taps = conv_weight.shape[1]
    rows = width // seq_count
    chips = seq_count // 2
    ids = base_ids.reshape(length // LANES, LANES)
    weight = jnp.transpose(conv_weight, (1, 0, 2)).reshape(taps * width, width)

    normed = norm_rows(trunk, ids, base_table, norm_gain[None])
    low, high = halos(normed, DILATION_STEP)
    hidden, dconv, turned_rows = conv_inner(normed, weight, trunk, grad, ids, base_table, rows)
    hidden, dconv, low_t, high_t = conv_edges(
        low, high, normed, weight, trunk, grad, ids, base_table, hidden, dconv, rows
    )

    swap = [(0, 1), (1, 0)]
    sent = grad_half((1 - core)[None], turned_rows, low_t, high_t, dconv)
    other_half = lax.ppermute(sent, "core", swap)
    accept_local = jnp.dot(hidden, accept_weight, preferred_element_type=F32).astype(BF16)
    accept_local, other_half = lax.optimization_barrier((accept_local, other_half))
    chip_half = grad_half(core[None], turned_rows, low_t, high_t, dconv, other_half)
    accept_local, accept_pos, donor_pos, chip_half = lax.optimization_barrier(
        (accept_local, accept_pos, donor_pos, chip_half)
    )
    pieces = lax.all_to_all(chip_half, CHIPS, 0, 0, tiled=True)

    accept_other = lax.ppermute(accept_local, "core", swap)
    slots = accept_pos.reshape(chips, 2, -1)
    mine, theirs = slots[:, :1], slots[:, 1:]
    slots = jnp.concatenate(
        [jnp.where(core == 0, mine, theirs), jnp.where(core == 0, theirs, mine)], axis=1
    )
    slots, place = chip_exchange(slots)
    counts = pair_counts[0]
    hot = (lax.dynamic_index_in_dim(counts, 2 * chip + 1 - core, 0) > slots.shape[2] // 2).astype(jnp.int32)
    served = serve(hot, place, slots, accept_local, accept_other)
    donor_emb = donor_rows(donor_pos.reshape(chips, 2, -1), hidden, donor_weight)

    pieces, served = lax.optimization_barrier((pieces, served))
    accepted = lax.all_to_all(served, CHIPS, 0, 0, tiled=True)

    own = jnp.sum(pieces.astype(F32), axis=0).reshape(taps * rows, width)
    total = dp_sum(own.T)
    weight_grad = jnp.transpose(total.reshape(-1, taps, rows), (2, 1, 0))
    junction_pairs = pairs(core[None], counts, donor_emb, accepted)[None]
    return (junction_pairs, weight_grad)


def solution(mesh):
    grid = Mesh(mesh.devices.reshape(8, 2, 2, 4, 2), AXES)
    return jax.shard_map(
        on_device,
        mesh=grid,
        in_specs=(
            P(DP, SEQ, None),
            P(DP, SEQ),
            P(),
            P(),
            P(),
            P(DP, SEQ, None),
            P(DP, SEQ),
            P(DP, SEQ),
            P(DP, SEQ),
            P(),
            P(),
        ),
        out_specs=(P(DP, SEQ, None), P(SEQ, None, DP)),
        check_vma=False,
    )
```

```python
import functools

import jax
import jax.numpy as jnp
from jax import lax
from jax.experimental import pallas as pl
from jax.experimental.pallas import tpu as pltpu
from jax.sharding import Mesh, PartitionSpec as P

DILATION_STEP = 256
AXES = ("z", "yl", "yh", "x", "core")
DP = ("z", "yl")
SEQ = ("yh", "x", "core")
CHIPS = ("yh", "x")
LANES = 128
MIB = 1024 * 1024
TILE = 256
BF16 = jnp.bfloat16
F32 = jnp.float32
GELU_A = 0.7978845608028654
GELU_B = 0.044715


def params(mib):
    return pltpu.CompilerParams(vmem_limit_bytes=mib * MIB)


def cost(flops, nbytes):
    return pl.CostEstimate(flops=flops, bytes_accessed=nbytes, transcendentals=0)


def in_hbm(x):
    return pltpu.with_memory_space_constraint(x, pltpu.HBM)


def dot(a, b):
    return jnp.dot(a, b, preferred_element_type=F32)


def across_lanes(row):
    return jnp.transpose(jnp.broadcast_to(row, (LANES, LANES)))


def summed_inputs(trunk, ids_ref, first, table_ref):
    rows, width = trunk.shape
    parts = []
    for block in range(rows // LANES):
        ids = across_lanes(ids_ref[pl.ds(first + block, 1), :])
        ids = jnp.concatenate([ids] * (width // LANES), axis=1)
        embedded = jnp.where(
            ids < 2,
            jnp.where(ids == 0, table_ref[0:1, :], table_ref[1:2, :]),
            jnp.where(ids == 2, table_ref[2:3, :], table_ref[3:4, :]),
        )
        parts.append(trunk[block * LANES : (block + 1) * LANES].astype(F32) + embedded)
    return jnp.concatenate(parts, axis=0)


def norm_kernel(core_ref, trunk_ref, ids_ref, table_ref, gain_ref, out_ref, near_ref, far_ref):
    i = pl.program_id(0)
    last = pl.num_programs(0) - 1
    per_chunk = trunk_ref.shape[0] // LANES
    inputs = summed_inputs(trunk_ref[...], ids_ref, i * per_chunk, table_ref)
    mean = jnp.mean(inputs * inputs, axis=-1, keepdims=True)
    normed = (inputs * lax.rsqrt(mean + 1e-06) * gain_ref[...][None, :]).astype(BF16)
    out_ref[...] = normed

    @pl.when(i == jnp.where(core_ref[0] == 0, last, 0))
    def _():
        near_ref[...] = normed

    @pl.when(i == jnp.where(core_ref[0] == 0, 0, last))
    def _():
        far_ref[...] = normed


def norm_rows(core, trunk, ids, table, gain):
    length, width = trunk.shape
    chunk = DILATION_STEP
    whole = lambda i, c: (0, 0)
    edge = jax.ShapeDtypeStruct((chunk, width), BF16)
    return pl.pallas_call(
        norm_kernel,
        grid_spec=pltpu.PrefetchScalarGridSpec(
            num_scalar_prefetch=1,
            grid=(length // chunk,),
            in_specs=[
                pl.BlockSpec((chunk, width), lambda i, c: (i, 0)),
                pl.BlockSpec(ids.shape, whole),
                pl.BlockSpec(table.shape, whole),
                pl.BlockSpec(gain.shape, lambda i, c: (0,)),
            ],
            out_specs=[
                pl.BlockSpec((chunk, width), lambda i, c: (i, 0)),
                pl.BlockSpec((chunk, width), whole),
                pl.BlockSpec((chunk, width), whole),
            ],
        ),
        out_shape=[jax.ShapeDtypeStruct((length, width), BF16), edge, edge],
        compiler_params=params(60),
        cost_estimate=cost(10 * length * width, 4 * length * width),
    )(core, trunk, ids, table, gain)


def gelu_parts(x):
    square = x * x
    t = jnp.tanh(GELU_A * x * (1.0 + GELU_B * square))
    cdf = 0.5 + 0.5 * t
    slope = cdf + (0.5 * GELU_A) * x * (1.0 - t * t) * (1.0 + (3 * GELU_B) * square)
    return x * cdf, slope


def turned(block, rows):
    width = block.shape[1]
    return jnp.transpose(block).reshape(width // (2 * rows), 2, rows, block.shape[0])


def conv_tile(left, mid, right, chunks, w_ref, trunk_refs, grad_refs, ids_ref, table_ref):
    out = dot(left, w_ref[0]) + dot(mid, w_ref[1]) + dot(right, w_ref[2])
    act, slope = gelu_parts(out)
    chunk = out.shape[0] // 2
    hidden, dconv = [], []
    for part in range(2):
        span = slice(part * chunk, (part + 1) * chunk)
        inputs = summed_inputs(trunk_refs[part][0], ids_ref, 2 * chunks[part], table_ref)
        hidden.append((inputs + act[span]).astype(BF16))
        dconv.append((grad_refs[part][0].astype(F32) * slope[span]).astype(BF16))
    return hidden, dconv


def inner_kernel(n_ref, w_ref, ta_ref, tb_ref, ga_ref, gb_ref, ids_ref, table_ref,
                 hidden_ref, dconv_ref, turned_ref, *, rows):
    chunk = DILATION_STEP
    two = 2 * chunk

    def tile():
        hidden, dconv = conv_tile(
            n_ref[:two], n_ref[chunk : chunk + two], n_ref[two:], (1, 2), w_ref,
            (ta_ref, tb_ref), (ga_ref, gb_ref), ids_ref, table_ref,
        )
        hidden_ref[...] = jnp.concatenate(hidden, axis=0)
        dconv_ref[...] = jnp.concatenate(dconv, axis=0)

    for step in range(2):

        @pl.when(pl.program_id(0) == step)
        def _():
            span = slice(step * two, (step + 1) * two)
            turned_ref[:, :, :, span] = turned(n_ref[span], rows)
            tile()

    pl.when(pl.program_id(0) == 2)(tile)


def conv_inner(normed, weight, trunk, grad, ids, table, rows):
    length, width = normed.shape
    chunk = DILATION_STEP
    groups = width // (2 * rows)
    whole = lambda n: (0, 0)
    part = lambda c: pl.BlockSpec((1, chunk, TILE), lambda n: (c, 0, n))
    out = pl.BlockSpec((2 * chunk, TILE), lambda n: (0, n))
    half = jax.ShapeDtypeStruct((2 * chunk, width), BF16)
    turned_shape = (groups, 2, rows, length)
    return pl.pallas_call(
        functools.partial(inner_kernel, rows=rows),
        grid=(width // TILE,),
        in_specs=[
            pl.BlockSpec(normed.shape, whole),
            pl.BlockSpec((3, width, TILE), lambda n: (0, 0, n)),
            part(1), part(2), part(1), part(2),
            pl.BlockSpec(ids.shape, whole),
            pl.BlockSpec((table.shape[0], TILE), lambda n: (0, n)),
        ],
        out_specs=[out, out, pl.BlockSpec(turned_shape, lambda n: (0, 0, 0, 0))],
        out_shape=[half, half, jax.ShapeDtypeStruct(turned_shape, BF16)],
        compiler_params=params(60),
        cost_estimate=cost(3 * length * width * width, 8 * length * width),
    )(normed, weight, trunk, trunk, grad, grad, ids, table)


def edge_kernel(core_ref, near_ref, far_ref, n_ref, w_ref, ta_ref, tb_ref, ga_ref, gb_ref, ids_ref, table_ref,
                inner_ref, turned_ref, hidden_ref, sent_ref, kept_ref, dconv_ref, low_t_ref, high_t_ref, *, rows):
    step = pl.program_id(0)
    chunk = near_ref.shape[0]
    length, width = n_ref.shape
    tiles = width // TILE
    first = core_ref[0] == 0
    part = lambda i: n_ref[i * chunk : (i + 1) * chunk]

    def conv(tile):
        low = jnp.where(first, far_ref[...], near_ref[...])
        high = jnp.where(first, near_ref[...], far_ref[...])
        left = jnp.concatenate([low, part(2)], axis=0)
        mid = jnp.concatenate([part(0), part(3)], axis=0)
        right = jnp.concatenate([part(1), high], axis=0)
        hidden, dconv = conv_tile(left, mid, right, (0, 3), w_ref, (ta_ref, tb_ref), (ga_ref, gb_ref),
                                  ids_ref, table_ref)
        hidden_ref[...] = jnp.concatenate(hidden, axis=0)
        span = slice(tile * TILE, (tile + 1) * TILE)
        dconv_ref[:chunk, span] = dconv[0]
        dconv_ref[3 * chunk :, span] = dconv[1]
        if tile == 0:
            low_t_ref[...] = turned(low, rows)
            dconv_ref[chunk : 3 * chunk] = inner_ref[...]
        if tile == 1:
            high_t_ref[...] = turned(high, rows)

    for tile in range(tiles):
        pl.when(step == tile)(functools.partial(conv, tile))

    for tap in range(3):

        @pl.when(step == tiles + tap)
        def _():
            if tap == 0:
                window = jnp.concatenate([low_t_ref[...], turned_ref[:, :, :, : length - chunk]], axis=3)
            elif tap == 1:
                window = turned_ref[...]
            else:
                window = jnp.concatenate([turned_ref[:, :, :, chunk:], high_t_ref[...]], axis=3)
            value = dot(window.reshape(width, length), dconv_ref[...])
            value = value.reshape(width // (2 * rows), 2, rows, width)
            kept_ref[:, 0] = jnp.where(first, value[:, 0], value[:, 1]).astype(BF16)
            sent_ref[:, 0] = jnp.where(first, value[:, 1], value[:, 0]).astype(BF16)


def edges_and_grad(core, near, far, normed, weight, trunk, grad, ids, table, inner, turned_rows):
    length, width = normed.shape
    chunk = near.shape[0]
    groups, _, rows, _ = turned_rows.shape
    tiles, taps = width // TILE, weight.shape[0]
    whole = lambda n, c: (0, 0)
    tile = lambda n: jnp.minimum(n, tiles - 1)
    part = lambda k: pl.BlockSpec((1, chunk, TILE), lambda n, c: (k, 0, tile(n)))
    block = pl.BlockSpec((groups, 1, rows, width), lambda n, c: (0, jnp.maximum(n - tiles, 0), 0, 0))
    piece = jax.ShapeDtypeStruct((groups, taps, rows, width), BF16)
    edge_t = pltpu.VMEM((groups, 2, rows, chunk), BF16)
    return pl.pallas_call(
        functools.partial(edge_kernel, rows=rows),
        grid_spec=pltpu.PrefetchScalarGridSpec(
            num_scalar_prefetch=1,
            grid=(tiles + taps,),
            in_specs=[
                pl.BlockSpec(near.shape, whole),
                pl.BlockSpec(far.shape, whole),
                pl.BlockSpec(normed.shape, whole),
                pl.BlockSpec((taps, width, TILE), lambda n, c: (0, 0, tile(n))),
                part(0), part(3), part(0), part(3),
                pl.BlockSpec(ids.shape, whole),
                pl.BlockSpec((table.shape[0], TILE), lambda n, c: (0, tile(n))),
                pl.BlockSpec(inner.shape, whole),
                pl.BlockSpec(turned_rows.shape, lambda n, c: (0, 0, 0, 0)),
            ],
            out_specs=[pl.BlockSpec((2 * chunk, TILE), lambda n, c: (0, tile(n))), block, block],
            scratch_shapes=[pltpu.VMEM((length, width), BF16), edge_t, edge_t],
        ),
        out_shape=[jax.ShapeDtypeStruct((2 * chunk, width), BF16), piece, piece],
        compiler_params=params(60),
        cost_estimate=cost(9 * length * width * width, 20 * length * width),
    )(core, near, far, normed, weight, trunk, trunk, grad, grad, ids, table, inner, turned_rows)


def table_kernel(inner_ref, outer_ref, weight_ref, after_ref, out_ref):
    del after_ref
    half = inner_ref.shape[0]
    out_ref[:half] = dot(inner_ref[...], weight_ref[...]).astype(BF16)
    out_ref[half:] = dot(outer_ref[...], weight_ref[...]).astype(BF16)


def projected(inner, outer, weight, after):
    half, width = inner.shape
    whole = lambda n: (0, 0)
    tile = lambda count: pl.BlockSpec((count, TILE), lambda n: (0, n))
    return pl.pallas_call(
        table_kernel,
        grid=(width // TILE,),
        in_specs=[
            pl.BlockSpec(inner.shape, whole),
            pl.BlockSpec(outer.shape, whole),
            tile(width),
            pl.BlockSpec(memory_space=pl.ANY),
        ],
        out_specs=tile(2 * half),
        out_shape=jax.ShapeDtypeStruct((2 * half, width), BF16),
        compiler_params=params(60),
        cost_estimate=cost(4 * half * width * width, 8 * half * width),
    )(inner, outer, weight, in_hbm(after))


def table_place(position):
    chunk = DILATION_STEP
    moved = jnp.where(position < 3 * chunk, position - chunk, position)
    return jnp.where(position < chunk, position + 2 * chunk, moved)


def join_kernel(kept_ref, got_ref, after_ref, out_ref):
    del after_ref
    out_ref[...] = (kept_ref[...].astype(F32) + got_ref[...].astype(F32)).astype(BF16)


def join(kept, got, after):
    groups, taps, rows, width = kept.shape
    block = pl.BlockSpec((groups // 4, taps, rows, width), lambda i: (i, 0, 0, 0))
    return pl.pallas_call(
        join_kernel,
        grid=(4,),
        in_specs=[block, block, pl.BlockSpec(memory_space=pl.ANY)],
        out_specs=block,
        out_shape=jax.ShapeDtypeStruct(kept.shape, BF16),
        compiler_params=params(8),
        cost_estimate=cost(kept.size, 6 * kept.size),
    )(in_hbm(kept), got, in_hbm(after))


def selected(index_rows, table_ref):
    lane = lax.broadcasted_iota(jnp.int32, (LANES, LANES), 1)
    picks = []
    for row in index_rows:
        index = across_lanes(table_place(row))
        picks.append(
            jnp.concatenate(
                [
                    jnp.where(index == lane + b * LANES, 1.0, 0.0).astype(BF16)
                    for b in range(table_ref.shape[0] // LANES)
                ],
                axis=1,
            )
        )
    return dot(jnp.concatenate(picks, axis=0), table_ref[...]).astype(BF16)


def serve_kernel(chip_ref, hot_ref, index_ref, own_ref, other_ref, after_ref, out_ref):
    del after_ref
    half = LANES // 2
    per = out_ref.shape[0]
    chip, core = chip_ref[0], chip_ref[1]
    sources = []
    for q in range(per):
        apart = jnp.bitwise_xor(chip, pl.program_id(0) * per + q)
        sources.append(apart // 4 + apart % 4 // 2 * 2 + apart % 2 * 4)
    asked = lambda k: [index_ref[source, pl.ds(2 * chip + k, 1), :] for source in sources]
    own = selected(asked(core), own_ref)
    other = selected(asked(1 - core), other_ref)
    hot = hot_ref[0] != 0
    for q in range(per):
        low, high = q * LANES, q * LANES + half
        out_ref[q, 0] = own[low:high]
        out_ref[q, 1] = other[low:high]

    @pl.when(jnp.logical_not(hot))
    def _():
        for q in range(per):
            out_ref[q, 2] = own[q * LANES + half : (q + 1) * LANES]

    @pl.when(hot)
    def _():
        for q in range(per):
            out_ref[q, 2] = other[q * LANES + half : (q + 1) * LANES]


def serve(chip, hot, index, own, other, after):
    groups = index.shape[0]
    width = own.shape[1]
    per = 4
    whole = lambda q, c, h: (0, 0)
    return pl.pallas_call(
        serve_kernel,
        grid_spec=pltpu.PrefetchScalarGridSpec(
            num_scalar_prefetch=2,
            grid=(groups // per,),
            in_specs=[
                pl.BlockSpec(index.shape, lambda q, c, h: (0, 0, 0)),
                pl.BlockSpec(own.shape, whole),
                pl.BlockSpec(other.shape, whole),
                pl.BlockSpec(memory_space=pl.ANY),
            ],
            out_specs=pl.BlockSpec((per, 3, LANES // 2, width), lambda q, c, h: (q, 0, 0, 0)),
        ),
        out_shape=jax.ShapeDtypeStruct((groups, 3, LANES // 2, width), BF16),
        compiler_params=params(60),
        cost_estimate=cost(4 * groups * LANES * own.shape[0] * width, 8 * own.size),
    )(chip, hot, index, own, other, in_hbm(after))


def donor_kernel(index_ref, table_ref, after_ref, out_ref):
    del after_ref
    per = out_ref.shape[0] // LANES
    first = pl.program_id(0) * per
    out_ref[...] = selected([index_ref[pl.ds(first + r, 1), :] for r in range(per)], table_ref)


def donor_rows(index, table, after):
    count = index.shape[0]
    width = table.shape[1]
    per = 4
    whole = lambda q: (0, 0)
    return pl.pallas_call(
        donor_kernel,
        grid=(count // per,),
        in_specs=[
            pl.BlockSpec(index.shape, whole),
            pl.BlockSpec(table.shape, whole),
            pl.BlockSpec(memory_space=pl.ANY),
        ],
        out_specs=pl.BlockSpec((per * LANES, width), lambda q: (q, 0)),
        out_shape=jax.ShapeDtypeStruct((count * LANES, width), BF16),
        compiler_params=params(60),
        cost_estimate=cost(2 * count * LANES * table.shape[0] * width, 10 * table.size),
    )(index, table, in_hbm(after))


def pair_kernel(core_ref, counts_ref, donor_ref, accepted_ref, out_ref):
    half = LANES // 2
    per = accepted_ref.shape[0]
    slot = lax.broadcasted_iota(jnp.int32, (half, LANES), 0)
    copies = out_ref.shape[1] // LANES
    for q in range(per):
        group = pl.program_id(0) * per + q
        for owner_core in range(2):
            count = counts_ref[2 * group + owner_core]
            place = lax.rem(core_ref[0] + owner_core, 2)
            for part, source in enumerate((place, 2)):
                at = (2 * q + owner_core) * LANES + part * half
                mask = jnp.where(slot + part * half < count, 1.0, 0.0).astype(BF16)
                mask = jnp.concatenate([mask] * copies, axis=1)
                out_ref[at : at + half] = accepted_ref[q, source] * donor_ref[at : at + half] * mask


def pairs(core, counts, donor, accepted):
    groups = accepted.shape[0]
    width = donor.shape[1]
    per = 2
    rows = pl.BlockSpec((2 * per * LANES, width), lambda q, c, n: (q, 0))
    return pl.pallas_call(
        pair_kernel,
        grid_spec=pltpu.PrefetchScalarGridSpec(
            num_scalar_prefetch=2,
            grid=(groups // per,),
            in_specs=[rows, pl.BlockSpec((per,) + accepted.shape[1:], lambda q, c, n: (q, 0, 0, 0))],
            out_specs=rows,
        ),
        out_shape=jax.ShapeDtypeStruct(donor.shape, BF16),
        compiler_params=params(12),
        cost_estimate=cost(2 * donor.size, 6 * donor.size),
    )(core, counts, in_hbm(donor), accepted)


def spread_kernel(z_ref, pieces_ref, *refs):
    outs, scratch = refs[:-1], refs[-1]
    chips, taps, rows, width = pieces_ref.shape
    total = pieces_ref[0].astype(F32)
    for i in range(1, chips):
        total = total + pieces_ref[i].astype(F32)
    scratch[...] = jnp.transpose(total.reshape(taps * rows, width))
    count = len(outs)
    size = width // count
    for step, out in enumerate(outs):
        start = pl.multiple_of(lax.rem(z_ref[0] + step, count) * size, size)
        out[...] = scratch[pl.ds(start, size), :].astype(out.dtype)


def spread(z, pieces, count):
    chips, taps, rows, width = pieces.shape
    shape = (width // count, taps * rows)
    return pl.pallas_call(
        spread_kernel,
        grid_spec=pltpu.PrefetchScalarGridSpec(
            num_scalar_prefetch=1,
            grid=(1,),
            in_specs=[pl.BlockSpec(pieces.shape, lambda i, z: (0, 0, 0, 0))],
            out_specs=[pl.BlockSpec(shape, lambda i, z: (0, 0))] * count,
            scratch_shapes=[pltpu.VMEM((width, taps * rows), F32)],
        ),
        out_shape=[jax.ShapeDtypeStruct(shape, BF16 if k else F32) for k in range(count)],
        compiler_params=params(12),
        cost_estimate=cost(2 * pieces.size, 3 * pieces.size),
    )(z, pieces)


def gather_kernel(yl_ref, own_ref, *refs):
    got, (kept_ref, sent_ref) = refs[:-2], refs[-2:]
    half = kept_ref.shape[0]

    def total(start):
        value = own_ref[start : start + half]
        for ref in got:
            value = value + ref[start : start + half].astype(F32)
        return value

    for yl in range(2):

        @pl.when(yl_ref[0] == yl)
        def _():
            kept_ref[...] = total(yl * half)
            sent_ref[...] = total((1 - yl) * half).astype(BF16)


def gathered(yl, own, got):
    rows, width = own.shape
    whole = lambda i, y: (0, 0)
    full = pl.BlockSpec(own.shape, whole)
    half = pl.BlockSpec((rows // 2, width), whole)
    return pl.pallas_call(
        gather_kernel,
        grid_spec=pltpu.PrefetchScalarGridSpec(
            num_scalar_prefetch=1, grid=(1,), in_specs=[full] * (1 + len(got)), out_specs=[half, half]
        ),
        out_shape=[
            jax.ShapeDtypeStruct((rows // 2, width), F32),
            jax.ShapeDtypeStruct((rows // 2, width), BF16),
        ],
        compiler_params=params(8),
        cost_estimate=cost(8 * own.size, 20 * own.size),
    )(yl, own, *got)


def final_kernel(kept_ref, got_ref, out_ref):
    total = kept_ref[...] + got_ref[...].astype(F32)
    out_ref[...] = jnp.transpose(total).reshape(out_ref.shape)


def final_grad(kept, got, taps):
    cols, width = kept.shape
    return pl.pallas_call(
        final_kernel,
        out_shape=jax.ShapeDtypeStruct((taps, width // taps, cols), F32),
        compiler_params=params(8),
    )(kept, got)


def dp_sum(outs, taps):
    nz = len(outs)
    got = [
        lax.ppermute(outs[step], "z", [(i, (i + step) % nz) for i in range(nz)])
        for step in range(1, nz)
    ]
    kept, sent = gathered(lax.axis_index("yl")[None], outs[0], got)
    return final_grad(kept, lax.ppermute(sent, "yl", [(0, 1), (1, 0)]), taps)


def on_device(
    trunk_acts,
    base_ids,
    base_table,
    norm_gain,
    conv_weight,
    grad_out,
    donor_pos,
    accept_pos,
    pair_counts,
    donor_weight,
    accept_weight,
):
    core = lax.axis_index("core")
    chip = lax.axis_index(CHIPS)
    trunk = trunk_acts[0]
    length, width = trunk.shape
    seq_count = lax.axis_size(SEQ)
    rows = width // seq_count
    chips = seq_count // 2
    ids = base_ids.reshape(length // LANES, LANES)
    weight = jnp.transpose(conv_weight, (1, 0, 2))
    swap = [(0, 1), (1, 0)]
    split = lambda v: v.reshape(length // DILATION_STEP, DILATION_STEP, width)
    core_id = core[None]

    def widened(slots, bit):
        other = lax.ppermute(slots, CHIPS, [(i, i ^ bit) for i in range(chips)])
        return jnp.concatenate([slots, other], axis=0)

    slots = widened(accept_pos.reshape(1, seq_count, -1), 4)
    normed, near, far = norm_rows(core_id, trunk, ids, base_table, norm_gain)
    slots = widened(slots, 2)
    borders = [(i, i + 1) for i in range(1, seq_count - 1, 2)]
    far = lax.ppermute(far, SEQ, borders + [(target, source) for source, target in borders])
    near = lax.ppermute(near, "core", swap)
    common = (normed, weight, split(trunk_acts), split(grad_out), ids, base_table)
    hidden_in, dconv_in, turned_rows = conv_inner(*common, rows)
    slots, dconv_in = lax.optimization_barrier((slots, dconv_in))
    slots = widened(slots, 1)
    near, far, slots = lax.optimization_barrier((near, far, slots))
    hidden_out, sent, kept = edges_and_grad(core_id, near, far, *common, dconv_in, turned_rows)
    got = lax.ppermute(sent, "core", swap)
    accept_local = projected(hidden_in, hidden_out, accept_weight, kept)
    chip_half = join(kept, got, accept_local)
    pieces = lax.all_to_all(chip_half, CHIPS, 0, 0, tiled=True)

    accept_other = lax.ppermute(accept_local, "core", swap)
    counts = pair_counts[0]
    hot = (lax.dynamic_index_in_dim(counts, 2 * chip + 1 - core, 0) > slots.shape[2] // 2).astype(jnp.int32)
    donor_table = projected(hidden_in, hidden_out, donor_weight, chip_half)
    donor_emb = donor_rows(donor_pos.reshape(2 * chips, -1), donor_table, chip_half)
    served = serve(jnp.stack([chip, core]), hot, slots, accept_local, accept_other, donor_emb)
    blocks = list(spread(lax.axis_index("z")[None], pieces, lax.axis_size("z")))
    served, blocks[0] = lax.optimization_barrier((served, blocks[0]))
    accepted = lax.all_to_all(served, CHIPS, 0, 0, tiled=True)
    weight_grad = jnp.transpose(dp_sum(blocks, conv_weight.shape[1]), (1, 0, 2))
    junction_pairs = pairs(core[None], counts, donor_emb, accepted)[None]
    return (junction_pairs, weight_grad)


def solution(mesh):
    grid = Mesh(mesh.devices.reshape(8, 2, 2, 4, 2), AXES)
    return jax.shard_map(
        on_device,
        mesh=grid,
        in_specs=(
            P(DP, SEQ, None),
            P(DP, SEQ),
            P(),
            P(),
            P(),
            P(DP, SEQ, None),
            P(DP, SEQ),
            P(DP, SEQ),
            P(DP, SEQ),
            P(),
            P(),
        ),
        out_specs=(P(DP, SEQ, None), P(SEQ, None, DP)),
        check_vma=False,
    )
```

```python
import functools

import jax
import jax.numpy as jnp
from jax import lax
from jax.experimental import pallas as pl
from jax.experimental.pallas import tpu as pltpu
from jax.sharding import Mesh, PartitionSpec as P

DILATION_STEP = 256
AXES = ("z", "yl", "yh", "x", "core")
DP = ("z", "yl")
SEQ = ("yh", "x", "core")
CHIPS = ("yh", "x")
LANES = 128
MIB = 1024 * 1024
TILE = 256
BF16 = jnp.bfloat16
F32 = jnp.float32
GELU_A = 0.7978845608028654
GELU_B = 0.044715


def params(mib):
    return pltpu.CompilerParams(vmem_limit_bytes=mib * MIB)


def cost(flops, nbytes):
    return pl.CostEstimate(flops=flops, bytes_accessed=nbytes, transcendentals=0)


def in_hbm(x):
    return pltpu.with_memory_space_constraint(x, pltpu.HBM)


def dot(a, b):
    return jnp.dot(a, b, preferred_element_type=F32)


def across_lanes(row):
    return jnp.transpose(jnp.broadcast_to(row, (LANES, LANES)))


def summed_inputs(trunk, ids_ref, first, table_ref):
    rows, width = trunk.shape
    parts = []
    for block in range(rows // LANES):
        ids = across_lanes(ids_ref[pl.ds(first + block, 1), :])
        ids = jnp.concatenate([ids] * (width // LANES), axis=1)
        embedded = jnp.where(
            ids < 2,
            jnp.where(ids == 0, table_ref[0:1, :], table_ref[1:2, :]),
            jnp.where(ids == 2, table_ref[2:3, :], table_ref[3:4, :]),
        )
        parts.append(trunk[block * LANES : (block + 1) * LANES].astype(F32) + embedded)
    return jnp.concatenate(parts, axis=0)


def norm_kernel(core_ref, trunk_ref, ids_ref, table_ref, gain_ref, out_ref, near_ref, far_ref):
    i = pl.program_id(0)
    last = pl.num_programs(0) - 1
    per_chunk = trunk_ref.shape[0] // LANES
    inputs = summed_inputs(trunk_ref[...], ids_ref, i * per_chunk, table_ref)
    mean = jnp.mean(inputs * inputs, axis=-1, keepdims=True)
    normed = (inputs * lax.rsqrt(mean + 1e-06) * gain_ref[...][None, :]).astype(BF16)
    out_ref[...] = normed

    @pl.when(i == jnp.where(core_ref[0] == 0, last, 0))
    def _():
        near_ref[...] = normed

    @pl.when(i == jnp.where(core_ref[0] == 0, 0, last))
    def _():
        far_ref[...] = normed


def norm_rows(core, trunk, ids, table, gain):
    length, width = trunk.shape
    chunk = DILATION_STEP
    whole = lambda i, c: (0, 0)
    edge = jax.ShapeDtypeStruct((chunk, width), BF16)
    return pl.pallas_call(
        norm_kernel,
        grid_spec=pltpu.PrefetchScalarGridSpec(
            num_scalar_prefetch=1,
            grid=(length // chunk,),
            in_specs=[
                pl.BlockSpec((chunk, width), lambda i, c: (i, 0)),
                pl.BlockSpec(ids.shape, whole),
                pl.BlockSpec(table.shape, whole),
                pl.BlockSpec(gain.shape, lambda i, c: (0,)),
            ],
            out_specs=[
                pl.BlockSpec((chunk, width), lambda i, c: (i, 0)),
                pl.BlockSpec((chunk, width), whole),
                pl.BlockSpec((chunk, width), whole),
            ],
        ),
        out_shape=[jax.ShapeDtypeStruct((length, width), BF16), edge, edge],
        compiler_params=params(60),
        cost_estimate=cost(10 * length * width, 4 * length * width),
    )(core, trunk, ids, table, gain)


def gelu_parts(x):
    square = x * x
    t = jnp.tanh(GELU_A * x * (1.0 + GELU_B * square))
    cdf = 0.5 + 0.5 * t
    slope = cdf + (0.5 * GELU_A) * x * (1.0 - t * t) * (1.0 + (3 * GELU_B) * square)
    return x * cdf, slope


def turned(block, rows):
    width = block.shape[1]
    return jnp.transpose(block).reshape(width // (2 * rows), 2, rows, block.shape[0])


def conv_tile(left, mid, right, chunks, w_ref, trunk_refs, grad_refs, ids_ref, table_ref):
    out = dot(left, w_ref[0]) + dot(mid, w_ref[1]) + dot(right, w_ref[2])
    act, slope = gelu_parts(out)
    chunk = out.shape[0] // 2
    hidden, dconv = [], []
    for part in range(2):
        span = slice(part * chunk, (part + 1) * chunk)
        inputs = summed_inputs(trunk_refs[part][0], ids_ref, 2 * chunks[part], table_ref)
        hidden.append((inputs + act[span]).astype(BF16))
        dconv.append((grad_refs[part][0].astype(F32) * slope[span]).astype(BF16))
    return hidden, dconv


def inner_kernel(n_ref, w_ref, ta_ref, tb_ref, ga_ref, gb_ref, ids_ref, table_ref,
                 hidden_ref, dconv_ref, turned_ref, *, rows):
    chunk = DILATION_STEP
    two = 2 * chunk

    def tile():
        hidden, dconv = conv_tile(
            n_ref[:two], n_ref[chunk : chunk + two], n_ref[two:], (1, 2), w_ref,
            (ta_ref, tb_ref), (ga_ref, gb_ref), ids_ref, table_ref,
        )
        hidden_ref[...] = jnp.concatenate(hidden, axis=0)
        dconv_ref[...] = jnp.concatenate(dconv, axis=0)

    for step in range(2):

        @pl.when(pl.program_id(0) == step)
        def _():
            span = slice(step * two, (step + 1) * two)
            turned_ref[:, :, :, span] = turned(n_ref[span], rows)
            tile()

    pl.when(pl.program_id(0) == 2)(tile)


def conv_inner(normed, weight, trunk, grad, ids, table, rows):
    length, width = normed.shape
    chunk = DILATION_STEP
    groups = width // (2 * rows)
    whole = lambda n: (0, 0)
    part = lambda c: pl.BlockSpec((1, chunk, TILE), lambda n: (c, 0, n))
    out = pl.BlockSpec((2 * chunk, TILE), lambda n: (0, n))
    half = jax.ShapeDtypeStruct((2 * chunk, width), BF16)
    turned_shape = (groups, 2, rows, length)
    return pl.pallas_call(
        functools.partial(inner_kernel, rows=rows),
        grid=(width // TILE,),
        in_specs=[
            pl.BlockSpec(normed.shape, whole),
            pl.BlockSpec((3, width, TILE), lambda n: (0, 0, n)),
            part(1), part(2), part(1), part(2),
            pl.BlockSpec(ids.shape, whole),
            pl.BlockSpec((table.shape[0], TILE), lambda n: (0, n)),
        ],
        out_specs=[out, out, pl.BlockSpec(turned_shape, lambda n: (0, 0, 0, 0))],
        out_shape=[half, half, jax.ShapeDtypeStruct(turned_shape, BF16)],
        compiler_params=params(60),
        cost_estimate=cost(3 * length * width * width, 8 * length * width),
    )(normed, weight, trunk, trunk, grad, grad, ids, table)


def edge_kernel(core_ref, near_ref, far_ref, n_ref, w_ref, ta_ref, tb_ref, ga_ref, gb_ref, ids_ref, table_ref,
                inner_ref, turned_ref, hidden_ref, sent_ref, kept_ref, dconv_ref, window_ref, sems, *, rows):
    step = pl.program_id(0)
    chunk = near_ref.shape[0]
    length, width = n_ref.shape
    tiles = width // TILE
    first = core_ref[0] == 0
    part = lambda i: n_ref[i * chunk : (i + 1) * chunk]
    fetches = [
        pltpu.make_async_copy(inner_ref, dconv_ref.at[chunk : 3 * chunk], sems.at[0]),
        pltpu.make_async_copy(turned_ref, window_ref.at[:, :, :, chunk : chunk + length], sems.at[1]),
    ]

    @pl.when(step == 0)
    def _():
        for fetch in fetches:
            fetch.start()

    def conv(tile):
        low = jnp.where(first, far_ref[...], near_ref[...])
        high = jnp.where(first, near_ref[...], far_ref[...])
        left = jnp.concatenate([low, part(2)], axis=0)
        mid = jnp.concatenate([part(0), part(3)], axis=0)
        right = jnp.concatenate([part(1), high], axis=0)
        hidden, dconv = conv_tile(left, mid, right, (0, 3), w_ref, (ta_ref, tb_ref), (ga_ref, gb_ref),
                                  ids_ref, table_ref)
        hidden_ref[...] = jnp.concatenate(hidden, axis=0)
        span = slice(tile * TILE, (tile + 1) * TILE)
        dconv_ref[:chunk, span] = dconv[0]
        dconv_ref[3 * chunk :, span] = dconv[1]
        if tile == 0:
            window_ref[:, :, :, :chunk] = turned(low, rows)
        if tile == 1:
            window_ref[:, :, :, chunk + length :] = turned(high, rows)

    for tile in range(tiles):
        pl.when(step == tile)(functools.partial(conv, tile))

    for tap in range(3):

        @pl.when(step == tiles + tap)
        def _():
            if tap == 0:
                for fetch in fetches:
                    fetch.wait()
            window = window_ref[:, :, :, tap * chunk : tap * chunk + length]
            value = dot(window.reshape(width, length), dconv_ref[...])
            value = value.reshape(width // (2 * rows), 2, rows, width)
            kept_ref[:, 0] = jnp.where(first, value[:, 0], value[:, 1]).astype(BF16)
            sent_ref[:, 0] = jnp.where(first, value[:, 1], value[:, 0]).astype(BF16)


def edges_and_grad(core, near, far, normed, weight, trunk, grad, ids, table, inner, turned_rows):
    length, width = normed.shape
    chunk = near.shape[0]
    groups, _, rows, _ = turned_rows.shape
    tiles, taps = width // TILE, weight.shape[0]
    whole = lambda n, c: (0, 0)
    tile = lambda n: jnp.minimum(n, tiles - 1)
    part = lambda k: pl.BlockSpec((1, chunk, TILE), lambda n, c: (k, 0, tile(n)))
    block = pl.BlockSpec((groups, 1, rows, width), lambda n, c: (0, jnp.maximum(n - tiles, 0), 0, 0))
    piece = jax.ShapeDtypeStruct((groups, taps, rows, width), BF16)
    return pl.pallas_call(
        functools.partial(edge_kernel, rows=rows),
        grid_spec=pltpu.PrefetchScalarGridSpec(
            num_scalar_prefetch=1,
            grid=(tiles + taps,),
            in_specs=[
                pl.BlockSpec(near.shape, whole),
                pl.BlockSpec(far.shape, whole),
                pl.BlockSpec(normed.shape, whole),
                pl.BlockSpec((taps, width, TILE), lambda n, c: (0, 0, tile(n))),
                part(0), part(3), part(0), part(3),
                pl.BlockSpec(ids.shape, whole),
                pl.BlockSpec((table.shape[0], TILE), lambda n, c: (0, tile(n))),
                pl.BlockSpec(memory_space=pl.ANY),
                pl.BlockSpec(memory_space=pl.ANY),
            ],
            out_specs=[pl.BlockSpec((2 * chunk, TILE), lambda n, c: (0, tile(n))), block, block],
            scratch_shapes=[
                pltpu.VMEM((length, width), BF16),
                pltpu.VMEM((groups, 2, rows, length + 2 * chunk), BF16),
                pltpu.SemaphoreType.DMA((2,)),
            ],
        ),
        out_shape=[
            pltpu.HBM((2 * chunk, width), BF16),
            pltpu.HBM(piece.shape, BF16),
            piece,
        ],
        compiler_params=params(34),
        cost_estimate=cost(9 * length * width * width, 20 * length * width),
    )(core, near, far, *[in_hbm(v) for v in (normed, weight, trunk, trunk, grad, grad, ids, table, inner, turned_rows)])


def table_kernel(inner_ref, outer_ref, weight_ref, after_ref, out_ref):
    del after_ref
    half = inner_ref.shape[0]
    out_ref[:half] = dot(inner_ref[...], weight_ref[...]).astype(BF16)
    out_ref[half:] = dot(outer_ref[...], weight_ref[...]).astype(BF16)


def projected(inner, outer, weight, after):
    half, width = inner.shape
    whole = lambda n: (0, 0)
    tile = lambda count: pl.BlockSpec((count, TILE), lambda n: (0, n))
    return pl.pallas_call(
        table_kernel,
        grid=(width // TILE,),
        in_specs=[
            pl.BlockSpec(inner.shape, whole),
            pl.BlockSpec(outer.shape, whole),
            tile(width),
            pl.BlockSpec(memory_space=pl.ANY),
        ],
        out_specs=tile(2 * half),
        out_shape=pltpu.HBM((2 * half, width), BF16),
        compiler_params=params(12),
        cost_estimate=cost(4 * half * width * width, 8 * half * width),
    )(in_hbm(inner), in_hbm(outer), in_hbm(weight), after)


def table_place(position):
    chunk = DILATION_STEP
    moved = jnp.where(position < 3 * chunk, position - chunk, position)
    return jnp.where(position < chunk, position + 2 * chunk, moved)


def join_kernel(kept_ref, got_ref, after_ref, out_ref):
    del after_ref
    out_ref[...] = (kept_ref[...].astype(F32) + got_ref[...].astype(F32)).astype(BF16)


def join(kept, got, after):
    groups, taps, rows, width = kept.shape
    block = pl.BlockSpec((groups // 4, taps, rows, width), lambda i: (i, 0, 0, 0))
    return pl.pallas_call(
        join_kernel,
        grid=(4,),
        in_specs=[block, block, pl.BlockSpec(memory_space=pl.ANY)],
        out_specs=block,
        out_shape=pltpu.HBM(kept.shape, BF16),
        compiler_params=params(8),
        cost_estimate=cost(kept.size, 6 * kept.size),
    )(kept, got, in_hbm(after))


def selected(index_rows, table_ref):
    lane = lax.broadcasted_iota(jnp.int32, (LANES, LANES), 1)
    picks = []
    for row in index_rows:
        index = across_lanes(table_place(row))
        picks.append(
            jnp.concatenate(
                [
                    jnp.where(index == lane + b * LANES, 1.0, 0.0).astype(BF16)
                    for b in range(table_ref.shape[0] // LANES)
                ],
                axis=1,
            )
        )
    return dot(jnp.concatenate(picks, axis=0), table_ref[...]).astype(BF16)


def serve_kernel(core_ref, hot_ref, index_ref, own_ref, other_ref, after_ref, out_ref):
    del after_ref
    half = LANES // 2
    per = out_ref.shape[0]
    core = core_ref[0]
    asked = lambda k: [index_ref[pl.program_id(0) * per + q, pl.ds(k, 1), :] for q in range(per)]
    own = selected(asked(core), own_ref)
    other = selected(asked(1 - core), other_ref)
    hot = hot_ref[0] != 0
    for q in range(per):
        low, high = q * LANES, q * LANES + half
        out_ref[q, 0] = own[low:high]
        out_ref[q, 1] = other[low:high]

    @pl.when(jnp.logical_not(hot))
    def _():
        for q in range(per):
            out_ref[q, 2] = own[q * LANES + half : (q + 1) * LANES]

    @pl.when(hot)
    def _():
        for q in range(per):
            out_ref[q, 2] = other[q * LANES + half : (q + 1) * LANES]


def serve(core, hot, index, own, other, after):
    groups = index.shape[0]
    width = own.shape[1]
    per = 4
    whole = lambda q, c, h: (0, 0)
    return pl.pallas_call(
        serve_kernel,
        grid_spec=pltpu.PrefetchScalarGridSpec(
            num_scalar_prefetch=2,
            grid=(groups // per,),
            in_specs=[
                pl.BlockSpec(index.shape, lambda q, c, h: (0, 0, 0)),
                pl.BlockSpec(own.shape, whole),
                pl.BlockSpec(other.shape, whole),
                pl.BlockSpec(memory_space=pl.ANY),
            ],
            out_specs=pl.BlockSpec((per, 3, LANES // 2, width), lambda q, c, h: (q, 0, 0, 0)),
        ),
        out_shape=jax.ShapeDtypeStruct((groups, 3, LANES // 2, width), BF16),
        compiler_params=params(60),
        cost_estimate=cost(4 * groups * LANES * own.shape[0] * width, 8 * own.size),
    )(core, hot, index, own, other, in_hbm(after))


def donor_kernel(index_ref, table_ref, after_ref, out_ref):
    del after_ref
    per = out_ref.shape[0] // LANES
    first = pl.program_id(0) * per
    out_ref[...] = selected([index_ref[pl.ds(first + r, 1), :] for r in range(per)], table_ref)


def donor_rows(index, table, after):
    count = index.shape[0]
    width = table.shape[1]
    per = 4
    whole = lambda q: (0, 0)
    return pl.pallas_call(
        donor_kernel,
        grid=(count // per,),
        in_specs=[
            pl.BlockSpec(index.shape, whole),
            pl.BlockSpec(table.shape, whole),
            pl.BlockSpec(memory_space=pl.ANY),
        ],
        out_specs=pl.BlockSpec((per * LANES, width), lambda q: (q, 0)),
        out_shape=jax.ShapeDtypeStruct((count * LANES, width), BF16),
        compiler_params=params(60),
        cost_estimate=cost(2 * count * LANES * table.shape[0] * width, 10 * table.size),
    )(index, table, in_hbm(after))


def pair_kernel(core_ref, counts_ref, donor_ref, accepted_ref, out_ref):
    half = LANES // 2
    per = accepted_ref.shape[0]
    slot = lax.broadcasted_iota(jnp.int32, (half, LANES), 0)
    copies = out_ref.shape[1] // LANES
    for q in range(per):
        group = pl.program_id(0) * per + q
        for owner_core in range(2):
            count = counts_ref[2 * group + owner_core]
            place = lax.rem(core_ref[0] + owner_core, 2)
            for part, source in enumerate((place, 2)):
                at = (2 * q + owner_core) * LANES + part * half
                mask = jnp.where(slot + part * half < count, 1.0, 0.0).astype(BF16)
                mask = jnp.concatenate([mask] * copies, axis=1)
                out_ref[at : at + half] = accepted_ref[q, source] * donor_ref[at : at + half] * mask


def pairs(core, counts, donor, accepted):
    groups = accepted.shape[0]
    width = donor.shape[1]
    per = 2
    rows = pl.BlockSpec((2 * per * LANES, width), lambda q, c, n: (q, 0))
    return pl.pallas_call(
        pair_kernel,
        grid_spec=pltpu.PrefetchScalarGridSpec(
            num_scalar_prefetch=2,
            grid=(groups // per,),
            in_specs=[rows, pl.BlockSpec((per,) + accepted.shape[1:], lambda q, c, n: (q, 0, 0, 0))],
            out_specs=rows,
        ),
        out_shape=jax.ShapeDtypeStruct(donor.shape, BF16),
        compiler_params=params(12),
        cost_estimate=cost(2 * donor.size, 6 * donor.size),
    )(core, counts, in_hbm(donor), accepted)


def spread_kernel(z_ref, pieces_ref, *refs):
    outs, scratch = refs[:-1], refs[-1]
    chips, taps, rows, width = pieces_ref.shape
    total = pieces_ref[0].astype(F32)
    for i in range(1, chips):
        total = total + pieces_ref[i].astype(F32)
    scratch[...] = jnp.transpose(total.reshape(taps * rows, width))
    count = len(outs)
    size = width // count
    for step, out in enumerate(outs):
        start = pl.multiple_of(lax.rem(z_ref[0] + step, count) * size, size)
        out[...] = scratch[pl.ds(start, size), :].astype(out.dtype)


def spread(z, pieces, count):
    chips, taps, rows, width = pieces.shape
    shape = (width // count, taps * rows)
    return pl.pallas_call(
        spread_kernel,
        grid_spec=pltpu.PrefetchScalarGridSpec(
            num_scalar_prefetch=1,
            grid=(1,),
            in_specs=[pl.BlockSpec(pieces.shape, lambda i, z: (0, 0, 0, 0))],
            out_specs=[pl.BlockSpec(shape, lambda i, z: (0, 0))] * count,
            scratch_shapes=[pltpu.VMEM((width, taps * rows), F32)],
        ),
        out_shape=[pltpu.HBM(shape, BF16 if k else F32) for k in range(count)],
        compiler_params=params(12),
        cost_estimate=cost(2 * pieces.size, 3 * pieces.size),
    )(z, pieces)


def gather_kernel(yl_ref, own_ref, *refs):
    got, (kept_ref, sent_ref) = refs[:-2], refs[-2:]
    half = kept_ref.shape[0]

    def total(start):
        value = own_ref[start : start + half]
        for ref in got:
            value = value + ref[start : start + half].astype(F32)
        return value

    for yl in range(2):

        @pl.when(yl_ref[0] == yl)
        def _():
            kept_ref[...] = total(yl * half)
            sent_ref[...] = total((1 - yl) * half).astype(BF16)


def gathered(yl, own, got):
    rows, width = own.shape
    whole = lambda i, y: (0, 0)
    full = pl.BlockSpec(own.shape, whole)
    half = pl.BlockSpec((rows // 2, width), whole)
    return pl.pallas_call(
        gather_kernel,
        grid_spec=pltpu.PrefetchScalarGridSpec(
            num_scalar_prefetch=1, grid=(1,), in_specs=[full] * (1 + len(got)), out_specs=[half, half]
        ),
        out_shape=[
            jax.ShapeDtypeStruct((rows // 2, width), F32),
            jax.ShapeDtypeStruct((rows // 2, width), BF16),
        ],
        compiler_params=params(8),
        cost_estimate=cost(8 * own.size, 20 * own.size),
    )(yl, own, *got)


def final_kernel(kept_ref, got_ref, out_ref):
    total = kept_ref[...] + got_ref[...].astype(F32)
    out_ref[...] = jnp.transpose(total).reshape(out_ref.shape)


def final_grad(kept, got, taps):
    cols, width = kept.shape
    return pl.pallas_call(
        final_kernel,
        out_shape=jax.ShapeDtypeStruct((taps, width // taps, cols), F32),
        compiler_params=params(8),
    )(kept, got)


def dp_sum(outs, taps):
    nz = len(outs)
    got = [
        lax.ppermute(outs[step], "z", [(i, (i + step) % nz) for i in range(nz)])
        for step in range(1, nz)
    ]
    kept, sent = gathered(lax.axis_index("yl")[None], outs[0], got)
    return final_grad(kept, lax.ppermute(sent, "yl", [(0, 1), (1, 0)]), taps)


def on_device(
    trunk_acts,
    base_ids,
    base_table,
    norm_gain,
    conv_weight,
    grad_out,
    donor_pos,
    accept_pos,
    pair_counts,
    donor_weight,
    accept_weight,
):
    core = lax.axis_index("core")
    chip = lax.axis_index(CHIPS)
    trunk = trunk_acts[0]
    length, width = trunk.shape
    seq_count = lax.axis_size(SEQ)
    rows = width // seq_count
    chips = seq_count // 2
    ids = base_ids.reshape(length // LANES, LANES)
    weight = jnp.transpose(conv_weight, (1, 0, 2))
    swap = [(0, 1), (1, 0)]
    split = lambda v: v.reshape(length // DILATION_STEP, DILATION_STEP, width)
    core_id = core[None]

    slots = lax.all_to_all(accept_pos.reshape(chips, 2, -1), CHIPS, 0, 0, tiled=True)
    normed, near, far = norm_rows(core_id, trunk, ids, base_table, norm_gain)
    borders = [(i, i + 1) for i in range(1, seq_count - 1, 2)]
    far = lax.ppermute(far, SEQ, borders + [(target, source) for source, target in borders])
    slots, near = lax.optimization_barrier((slots, near))
    near = lax.ppermute(near, "core", swap)
    common = (normed, weight, split(trunk_acts), split(grad_out), ids, base_table)
    hidden_in, dconv_in, turned_rows = conv_inner(*common, rows)
    hidden_out, sent, kept = edges_and_grad(core_id, near, far, *common, dconv_in, turned_rows)
    got = lax.ppermute(sent, "core", swap)
    accept_local = projected(hidden_in, hidden_out, accept_weight, kept)
    chip_half = join(kept, got, accept_local)
    pieces = lax.all_to_all(chip_half, CHIPS, 0, 0, tiled=True)

    accept_other = lax.ppermute(accept_local, "core", swap)
    counts = pair_counts[0]
    hot = (lax.dynamic_index_in_dim(counts, 2 * chip + 1 - core, 0) > slots.shape[2] // 2).astype(jnp.int32)
    donor_table = projected(hidden_in, hidden_out, donor_weight, chip_half)
    donor_emb = donor_rows(donor_pos.reshape(2 * chips, -1), donor_table, chip_half)
    served = serve(core_id, hot, slots, accept_local, accept_other, donor_emb)
    blocks = list(spread(lax.axis_index("z")[None], pieces, lax.axis_size("z")))
    served, blocks[0] = lax.optimization_barrier((served, blocks[0]))
    accepted = lax.all_to_all(served, CHIPS, 0, 0, tiled=True)
    weight_grad = jnp.transpose(dp_sum(blocks, conv_weight.shape[1]), (1, 0, 2))
    junction_pairs = pairs(core[None], counts, donor_emb, accepted)[None]
    return (junction_pairs, weight_grad)


def solution(mesh):
    grid = Mesh(mesh.devices.reshape(8, 2, 2, 4, 2), AXES)
    return jax.shard_map(
        on_device,
        mesh=grid,
        in_specs=(
            P(DP, SEQ, None),
            P(DP, SEQ),
            P(),
            P(),
            P(),
            P(DP, SEQ, None),
            P(DP, SEQ),
            P(DP, SEQ),
            P(DP, SEQ),
            P(),
            P(),
        ),
        out_specs=(P(DP, SEQ, None), P(SEQ, None, DP)),
        check_vma=False,
    )
```

```python
import functools

import jax
import jax.numpy as jnp
from jax import lax
from jax.experimental import pallas as pl
from jax.experimental.pallas import tpu as pltpu
from jax.sharding import Mesh, PartitionSpec as P

DILATION_STEP = 256
AXES = ("z", "yl", "yh", "x", "core")
DP = ("z", "yl")
SEQ = ("yh", "x", "core")
CHIPS = ("yh", "x")
LANES = 128
MIB = 1024 * 1024
TILE = 256
BF16 = jnp.bfloat16
F32 = jnp.float32
GELU_A = 0.7978845608028654
GELU_B = 0.044715


def params(mib):
    return pltpu.CompilerParams(vmem_limit_bytes=mib * MIB)


def cost(flops, nbytes):
    return pl.CostEstimate(flops=flops, bytes_accessed=nbytes, transcendentals=0)


def in_hbm(x):
    return pltpu.with_memory_space_constraint(x, pltpu.HBM)


def dot(a, b):
    return jnp.dot(a, b, preferred_element_type=F32)


def across_lanes(row):
    return jnp.transpose(jnp.broadcast_to(row, (LANES, LANES)))


def summed_inputs(trunk, ids_ref, first, table_ref):
    rows, width = trunk.shape
    parts = []
    for block in range(rows // LANES):
        ids = across_lanes(ids_ref[pl.ds(first + block, 1), :])
        ids = jnp.concatenate([ids] * (width // LANES), axis=1)
        embedded = jnp.where(
            ids < 2,
            jnp.where(ids == 0, table_ref[0:1, :], table_ref[1:2, :]),
            jnp.where(ids == 2, table_ref[2:3, :], table_ref[3:4, :]),
        )
        parts.append(trunk[block * LANES : (block + 1) * LANES].astype(F32) + embedded)
    return jnp.concatenate(parts, axis=0)


def norm_kernel(core_ref, trunk_ref, ids_ref, table_ref, gain_ref, out_ref, near_ref, far_ref):
    i = pl.program_id(0)
    last = pl.num_programs(0) - 1
    per_chunk = trunk_ref.shape[0] // LANES
    inputs = summed_inputs(trunk_ref[...], ids_ref, i * per_chunk, table_ref)
    mean = jnp.mean(inputs * inputs, axis=-1, keepdims=True)
    normed = (inputs * lax.rsqrt(mean + 1e-06) * gain_ref[...][None, :]).astype(BF16)
    out_ref[...] = normed
    chunk = near_ref.shape[0]
    edge = jnp.where(i == 0, normed[:chunk], normed[normed.shape[0] - chunk :])

    @pl.when(i == jnp.where(core_ref[0] == 0, last, 0))
    def _():
        near_ref[...] = edge

    @pl.when(i == jnp.where(core_ref[0] == 0, 0, last))
    def _():
        far_ref[...] = edge


def norm_rows(core, trunk, ids, table, gain):
    length, width = trunk.shape
    chunk = DILATION_STEP
    block = length // 2
    whole = lambda i, c: (0, 0)
    edge = jax.ShapeDtypeStruct((chunk, width), BF16)
    return pl.pallas_call(
        norm_kernel,
        grid_spec=pltpu.PrefetchScalarGridSpec(
            num_scalar_prefetch=1,
            grid=(length // block,),
            in_specs=[
                pl.BlockSpec((block, width), lambda i, c: (i, 0)),
                pl.BlockSpec(ids.shape, whole),
                pl.BlockSpec(table.shape, whole),
                pl.BlockSpec(gain.shape, lambda i, c: (0,)),
            ],
            out_specs=[
                pl.BlockSpec((block, width), lambda i, c: (i, 0)),
                pl.BlockSpec((chunk, width), whole),
                pl.BlockSpec((chunk, width), whole),
            ],
        ),
        out_shape=[jax.ShapeDtypeStruct((length, width), BF16), edge, edge],
        compiler_params=params(60),
        cost_estimate=cost(10 * length * width, 4 * length * width),
    )(core, trunk, ids, table, gain)


def gelu_parts(x):
    square = x * x
    t = jnp.tanh(GELU_A * x * (1.0 + GELU_B * square))
    cdf = 0.5 + 0.5 * t
    slope = cdf + (0.5 * GELU_A) * x * (1.0 - t * t) * (1.0 + (3 * GELU_B) * square)
    return x * cdf, slope


def turned(block, rows):
    width = block.shape[1]
    return jnp.transpose(block).reshape(width // (2 * rows), 2, rows, block.shape[0])


def conv_tile(left, mid, right, chunks, w_ref, trunk_refs, grad_refs, ids_ref, table_ref):
    out = dot(left, w_ref[0]) + dot(mid, w_ref[1]) + dot(right, w_ref[2])
    act, slope = gelu_parts(out)
    chunk = out.shape[0] // 2
    hidden, dconv = [], []
    for part in range(2):
        span = slice(part * chunk, (part + 1) * chunk)
        inputs = summed_inputs(trunk_refs[part][0], ids_ref, 2 * chunks[part], table_ref)
        hidden.append((inputs + act[span]).astype(BF16))
        dconv.append((grad_refs[part][0].astype(F32) * slope[span]).astype(BF16))
    return hidden, dconv


def inner_kernel(n_ref, w_ref, ta_ref, tb_ref, ga_ref, gb_ref, ids_ref, table_ref,
                 hidden_ref, dconv_ref, turned_ref, *, rows):
    chunk = DILATION_STEP
    two = 2 * chunk

    def tile():
        hidden, dconv = conv_tile(
            n_ref[:two], n_ref[chunk : chunk + two], n_ref[two:], (1, 2), w_ref,
            (ta_ref, tb_ref), (ga_ref, gb_ref), ids_ref, table_ref,
        )
        hidden_ref[...] = jnp.concatenate(hidden, axis=0)
        dconv_ref[...] = jnp.concatenate(dconv, axis=0)

    for step in range(2):

        @pl.when(pl.program_id(0) == step)
        def _():
            span = slice(step * two, (step + 1) * two)
            turned_ref[:, :, :, span] = turned(n_ref[span], rows)
            tile()

    pl.when(pl.program_id(0) == 2)(tile)


def conv_inner(normed, weight, trunk, grad, ids, table, rows):
    length, width = normed.shape
    chunk = DILATION_STEP
    groups = width // (2 * rows)
    whole = lambda n: (0, 0)
    part = lambda c: pl.BlockSpec((1, chunk, TILE), lambda n: (c, 0, n))
    out = pl.BlockSpec((2 * chunk, TILE), lambda n: (0, n))
    half = jax.ShapeDtypeStruct((2 * chunk, width), BF16)
    turned_shape = (groups, 2, rows, length)
    return pl.pallas_call(
        functools.partial(inner_kernel, rows=rows),
        grid=(width // TILE,),
        in_specs=[
            pl.BlockSpec(normed.shape, whole),
            pl.BlockSpec((3, width, TILE), lambda n: (0, 0, n)),
            part(1), part(2), part(1), part(2),
            pl.BlockSpec(ids.shape, whole),
            pl.BlockSpec((table.shape[0], TILE), lambda n: (0, n)),
        ],
        out_specs=[out, out, pl.BlockSpec(turned_shape, lambda n: (0, 0, 0, 0))],
        out_shape=[half, half, jax.ShapeDtypeStruct(turned_shape, BF16)],
        compiler_params=params(60),
        cost_estimate=cost(3 * length * width * width, 8 * length * width),
    )(normed, weight, trunk, trunk, grad, grad, ids, table)


def edge_kernel(core_ref, near_ref, far_ref, n_ref, w_ref, ta_ref, tb_ref, ga_ref, gb_ref, ids_ref, table_ref,
                inner_ref, turned_ref, hidden_ref, sent_ref, kept_ref, dconv_ref, window_ref, sems, *, rows):
    step = pl.program_id(0)
    chunk = near_ref.shape[0]
    length, width = n_ref.shape
    tiles = width // TILE
    first = core_ref[0] == 0
    part = lambda i: n_ref[i * chunk : (i + 1) * chunk]
    fetches = [
        pltpu.make_async_copy(inner_ref, dconv_ref.at[chunk : 3 * chunk], sems.at[0]),
        pltpu.make_async_copy(turned_ref, window_ref.at[:, :, :, chunk : chunk + length], sems.at[1]),
    ]

    @pl.when(step == 0)
    def _():
        for fetch in fetches:
            fetch.start()

    def conv(tile):
        low = jnp.where(first, far_ref[...], near_ref[...])
        high = jnp.where(first, near_ref[...], far_ref[...])
        left = jnp.concatenate([low, part(2)], axis=0)
        mid = jnp.concatenate([part(0), part(3)], axis=0)
        right = jnp.concatenate([part(1), high], axis=0)
        hidden, dconv = conv_tile(left, mid, right, (0, 3), w_ref, (ta_ref, tb_ref), (ga_ref, gb_ref),
                                  ids_ref, table_ref)
        hidden_ref[...] = jnp.concatenate(hidden, axis=0)
        span = slice(tile * TILE, (tile + 1) * TILE)
        dconv_ref[:chunk, span] = dconv[0]
        dconv_ref[3 * chunk :, span] = dconv[1]
        if tile == 0:
            window_ref[:, :, :, :chunk] = turned(low, rows)
        if tile == 1:
            window_ref[:, :, :, chunk + length :] = turned(high, rows)

    for tile in range(tiles):
        pl.when(step == tile)(functools.partial(conv, tile))

    for tap in range(3):

        @pl.when(step == tiles + tap)
        def _():
            if tap == 0:
                for fetch in fetches:
                    fetch.wait()
            window = window_ref[:, :, :, tap * chunk : tap * chunk + length]
            value = dot(window.reshape(width, length), dconv_ref[...])
            value = value.reshape(width // (2 * rows), 2, rows, width)
            kept_ref[:, 0] = jnp.where(first, value[:, 0], value[:, 1]).astype(BF16)
            sent_ref[:, 0] = jnp.where(first, value[:, 1], value[:, 0]).astype(BF16)


def edges_and_grad(core, near, far, normed, weight, trunk, grad, ids, table, inner, turned_rows):
    length, width = normed.shape
    chunk = near.shape[0]
    groups, _, rows, _ = turned_rows.shape
    tiles, taps = width // TILE, weight.shape[0]
    whole = lambda n, c: (0, 0)
    tile = lambda n: jnp.minimum(n, tiles - 1)
    part = lambda k: pl.BlockSpec((1, chunk, TILE), lambda n, c: (k, 0, tile(n)))
    block = pl.BlockSpec((groups, 1, rows, width), lambda n, c: (0, jnp.maximum(n - tiles, 0), 0, 0))
    piece = jax.ShapeDtypeStruct((groups, taps, rows, width), BF16)
    return pl.pallas_call(
        functools.partial(edge_kernel, rows=rows),
        grid_spec=pltpu.PrefetchScalarGridSpec(
            num_scalar_prefetch=1,
            grid=(tiles + taps,),
            in_specs=[
                pl.BlockSpec(near.shape, whole),
                pl.BlockSpec(far.shape, whole),
                pl.BlockSpec(normed.shape, whole),
                pl.BlockSpec((taps, width, TILE), lambda n, c: (0, 0, tile(n))),
                part(0), part(3), part(0), part(3),
                pl.BlockSpec(ids.shape, whole),
                pl.BlockSpec((table.shape[0], TILE), lambda n, c: (0, tile(n))),
                pl.BlockSpec(memory_space=pl.ANY),
                pl.BlockSpec(memory_space=pl.ANY),
            ],
            out_specs=[pl.BlockSpec((2 * chunk, TILE), lambda n, c: (0, tile(n))), block, block],
            scratch_shapes=[
                pltpu.VMEM((length, width), BF16),
                pltpu.VMEM((groups, 2, rows, length + 2 * chunk), BF16),
                pltpu.SemaphoreType.DMA((2,)),
            ],
        ),
        out_shape=[
            pltpu.HBM((2 * chunk, width), BF16),
            pltpu.HBM(piece.shape, BF16),
            piece,
        ],
        compiler_params=params(34),
        cost_estimate=cost(9 * length * width * width, 20 * length * width),
    )(core, near, far, *[in_hbm(v) for v in (normed, weight, trunk, trunk, grad, grad, ids, table, inner, turned_rows)])


def table_kernel(inner_ref, outer_ref, weight_ref, after_ref, out_ref):
    del after_ref
    half = inner_ref.shape[0]
    out_ref[:half] = dot(inner_ref[...], weight_ref[...]).astype(BF16)
    out_ref[half:] = dot(outer_ref[...], weight_ref[...]).astype(BF16)


def projected(inner, outer, weight, after):
    half, width = inner.shape
    whole = lambda n: (0, 0)
    tile = lambda count: pl.BlockSpec((count, TILE), lambda n: (0, n))
    return pl.pallas_call(
        table_kernel,
        grid=(width // TILE,),
        in_specs=[
            pl.BlockSpec(inner.shape, whole),
            pl.BlockSpec(outer.shape, whole),
            tile(width),
            pl.BlockSpec(memory_space=pl.ANY),
        ],
        out_specs=tile(2 * half),
        out_shape=pltpu.HBM((2 * half, width), BF16),
        compiler_params=params(12),
        cost_estimate=cost(4 * half * width * width, 8 * half * width),
    )(in_hbm(inner), in_hbm(outer), in_hbm(weight), after)


def table_place(position):
    chunk = DILATION_STEP
    moved = jnp.where(position < 3 * chunk, position - chunk, position)
    return jnp.where(position < chunk, position + 2 * chunk, moved)


def join_kernel(kept_ref, got_ref, after_ref, out_ref):
    del after_ref
    out_ref[...] = (kept_ref[...].astype(F32) + got_ref[...].astype(F32)).astype(BF16)


def join(kept, got, after):
    groups, taps, rows, width = kept.shape
    block = pl.BlockSpec((groups // 4, taps, rows, width), lambda i: (i, 0, 0, 0))
    return pl.pallas_call(
        join_kernel,
        grid=(4,),
        in_specs=[block, block, pl.BlockSpec(memory_space=pl.ANY)],
        out_specs=block,
        out_shape=pltpu.HBM(kept.shape, BF16),
        compiler_params=params(8),
        cost_estimate=cost(kept.size, 6 * kept.size),
    )(kept, got, in_hbm(after))


def selected(index_rows, table_ref):
    lane = lax.broadcasted_iota(jnp.int32, (LANES, LANES), 1)
    picks = []
    for row in index_rows:
        index = across_lanes(table_place(row))
        picks.append(
            jnp.concatenate(
                [
                    jnp.where(index == lane + b * LANES, 1.0, 0.0).astype(BF16)
                    for b in range(table_ref.shape[0] // LANES)
                ],
                axis=1,
            )
        )
    return dot(jnp.concatenate(picks, axis=0), table_ref[...]).astype(BF16)


def serve_kernel(core_ref, hot_ref, index_ref, own_ref, other_ref, after_ref, out_ref):
    del after_ref
    half = LANES // 2
    per = out_ref.shape[0]
    core = core_ref[0]
    asked = lambda k: [index_ref[pl.program_id(0) * per + q, pl.ds(k, 1), :] for q in range(per)]
    own = selected(asked(core), own_ref)
    other = selected(asked(1 - core), other_ref)
    hot = hot_ref[0] != 0
    for q in range(per):
        low, high = q * LANES, q * LANES + half
        out_ref[q, 0] = own[low:high]
        out_ref[q, 1] = other[low:high]

    @pl.when(jnp.logical_not(hot))
    def _():
        for q in range(per):
            out_ref[q, 2] = own[q * LANES + half : (q + 1) * LANES]

    @pl.when(hot)
    def _():
        for q in range(per):
            out_ref[q, 2] = other[q * LANES + half : (q + 1) * LANES]


def serve(core, hot, index, own, other, after):
    groups = index.shape[0]
    width = own.shape[1]
    per = 4
    whole = lambda q, c, h: (0, 0)
    return pl.pallas_call(
        serve_kernel,
        grid_spec=pltpu.PrefetchScalarGridSpec(
            num_scalar_prefetch=2,
            grid=(groups // per,),
            in_specs=[
                pl.BlockSpec(index.shape, lambda q, c, h: (0, 0, 0)),
                pl.BlockSpec(own.shape, whole),
                pl.BlockSpec(other.shape, whole),
                pl.BlockSpec(memory_space=pl.ANY),
            ],
            out_specs=pl.BlockSpec((per, 3, LANES // 2, width), lambda q, c, h: (q, 0, 0, 0)),
        ),
        out_shape=jax.ShapeDtypeStruct((groups, 3, LANES // 2, width), BF16),
        compiler_params=params(60),
        cost_estimate=cost(4 * groups * LANES * own.shape[0] * width, 8 * own.size),
    )(core, hot, index, own, other, in_hbm(after))


def donor_kernel(index_ref, table_ref, after_ref, out_ref):
    del after_ref
    per = out_ref.shape[0] // LANES
    first = pl.program_id(0) * per
    out_ref[...] = selected([index_ref[pl.ds(first + r, 1), :] for r in range(per)], table_ref)


def donor_rows(index, table, after):
    count = index.shape[0]
    width = table.shape[1]
    per = 4
    whole = lambda q: (0, 0)
    return pl.pallas_call(
        donor_kernel,
        grid=(count // per,),
        in_specs=[
            pl.BlockSpec(index.shape, whole),
            pl.BlockSpec(table.shape, whole),
            pl.BlockSpec(memory_space=pl.ANY),
        ],
        out_specs=pl.BlockSpec((per * LANES, width), lambda q: (q, 0)),
        out_shape=jax.ShapeDtypeStruct((count * LANES, width), BF16),
        compiler_params=params(60),
        cost_estimate=cost(2 * count * LANES * table.shape[0] * width, 10 * table.size),
    )(index, table, in_hbm(after))


def pair_kernel(core_ref, counts_ref, donor_ref, accepted_ref, out_ref):
    half = LANES // 2
    per = accepted_ref.shape[0]
    slot = lax.broadcasted_iota(jnp.int32, (half, LANES), 0)
    copies = out_ref.shape[1] // LANES
    for q in range(per):
        group = pl.program_id(0) * per + q
        for owner_core in range(2):
            count = counts_ref[2 * group + owner_core]
            place = lax.rem(core_ref[0] + owner_core, 2)
            for part, source in enumerate((place, 2)):
                at = (2 * q + owner_core) * LANES + part * half
                mask = jnp.where(slot + part * half < count, 1.0, 0.0).astype(BF16)
                mask = jnp.concatenate([mask] * copies, axis=1)
                out_ref[at : at + half] = accepted_ref[q, source] * donor_ref[at : at + half] * mask


def pairs(core, counts, donor, accepted):
    groups = accepted.shape[0]
    width = donor.shape[1]
    per = 4
    rows = pl.BlockSpec((2 * per * LANES, width), lambda q, c, n: (q, 0))
    return pl.pallas_call(
        pair_kernel,
        grid_spec=pltpu.PrefetchScalarGridSpec(
            num_scalar_prefetch=2,
            grid=(groups // per,),
            in_specs=[rows, pl.BlockSpec((per,) + accepted.shape[1:], lambda q, c, n: (q, 0, 0, 0))],
            out_specs=rows,
        ),
        out_shape=jax.ShapeDtypeStruct(donor.shape, BF16),
        compiler_params=params(16),
        cost_estimate=cost(2 * donor.size, 6 * donor.size),
    )(core, counts, in_hbm(donor), accepted)


def spread_kernel(z_ref, pieces_ref, *refs):
    outs, scratch = refs[:-1], refs[-1]
    chips, taps, rows, width = pieces_ref.shape
    total = pieces_ref[0].astype(F32)
    for i in range(1, chips):
        total = total + pieces_ref[i].astype(F32)
    scratch[...] = jnp.transpose(total.reshape(taps * rows, width))
    count = len(outs)
    size = width // count
    for step, out in enumerate(outs):
        start = pl.multiple_of(lax.rem(z_ref[0] + step, count) * size, size)
        out[...] = scratch[pl.ds(start, size), :].astype(out.dtype)


def spread(z, pieces, count):
    chips, taps, rows, width = pieces.shape
    shape = (width // count, taps * rows)
    return pl.pallas_call(
        spread_kernel,
        grid_spec=pltpu.PrefetchScalarGridSpec(
            num_scalar_prefetch=1,
            grid=(1,),
            in_specs=[pl.BlockSpec(pieces.shape, lambda i, z: (0, 0, 0, 0))],
            out_specs=[pl.BlockSpec(shape, lambda i, z: (0, 0))] * count,
            scratch_shapes=[pltpu.VMEM((width, taps * rows), F32)],
        ),
        out_shape=[pltpu.HBM(shape, BF16 if k else F32) for k in range(count)],
        compiler_params=params(12),
        cost_estimate=cost(2 * pieces.size, 3 * pieces.size),
    )(z, pieces)


def gather_kernel(yl_ref, own_ref, *refs):
    got, (kept_ref, sent_ref) = refs[:-2], refs[-2:]
    half = kept_ref.shape[0]

    def total(start):
        value = own_ref[start : start + half]
        for ref in got:
            value = value + ref[start : start + half].astype(F32)
        return value

    for yl in range(2):

        @pl.when(yl_ref[0] == yl)
        def _():
            kept_ref[...] = total(yl * half)
            sent_ref[...] = total((1 - yl) * half).astype(BF16)


def gathered(yl, own, got):
    rows, width = own.shape
    whole = lambda i, y: (0, 0)
    full = pl.BlockSpec(own.shape, whole)
    half = pl.BlockSpec((rows // 2, width), whole)
    return pl.pallas_call(
        gather_kernel,
        grid_spec=pltpu.PrefetchScalarGridSpec(
            num_scalar_prefetch=1, grid=(1,), in_specs=[full] * (1 + len(got)), out_specs=[half, half]
        ),
        out_shape=[
            jax.ShapeDtypeStruct((rows // 2, width), F32),
            jax.ShapeDtypeStruct((rows // 2, width), BF16),
        ],
        compiler_params=params(8),
        cost_estimate=cost(8 * own.size, 20 * own.size),
    )(yl, own, *got)


def final_kernel(kept_ref, got_ref, out_ref):
    total = kept_ref[...] + got_ref[...].astype(F32)
    out_ref[...] = jnp.transpose(total).reshape(out_ref.shape)


def final_grad(kept, got, taps):
    cols, width = kept.shape
    return pl.pallas_call(
        final_kernel,
        out_shape=jax.ShapeDtypeStruct((taps, width // taps, cols), F32),
        compiler_params=params(8),
    )(kept, got)


def dp_sum(outs, taps):
    nz = len(outs)
    got = [
        lax.ppermute(outs[step], "z", [(i, (i + step) % nz) for i in range(nz)])
        for step in range(1, nz)
    ]
    kept, sent = gathered(lax.axis_index("yl")[None], outs[0], got)
    return final_grad(kept, lax.ppermute(sent, "yl", [(0, 1), (1, 0)]), taps)


def on_device(
    trunk_acts,
    base_ids,
    base_table,
    norm_gain,
    conv_weight,
    grad_out,
    donor_pos,
    accept_pos,
    pair_counts,
    donor_weight,
    accept_weight,
):
    core = lax.axis_index("core")
    chip = lax.axis_index(CHIPS)
    trunk = trunk_acts[0]
    length, width = trunk.shape
    seq_count = lax.axis_size(SEQ)
    rows = width // seq_count
    chips = seq_count // 2
    ids = base_ids.reshape(length // LANES, LANES)
    weight = jnp.transpose(conv_weight, (1, 0, 2))
    swap = [(0, 1), (1, 0)]
    split = lambda v: v.reshape(length // DILATION_STEP, DILATION_STEP, width)
    core_id = core[None]

    slots = lax.all_to_all(accept_pos.reshape(chips, 2, -1), CHIPS, 0, 0, tiled=True)
    normed, near, far = norm_rows(core_id, trunk, ids, base_table, norm_gain)
    borders = [(i, i + 1) for i in range(1, seq_count - 1, 2)]
    far = lax.ppermute(far, SEQ, borders + [(target, source) for source, target in borders])
    slots, near = lax.optimization_barrier((slots, near))
    near = lax.ppermute(near, "core", swap)
    common = (normed, weight, split(trunk_acts), split(grad_out), ids, base_table)
    hidden_in, dconv_in, turned_rows = conv_inner(*common, rows)
    hidden_out, sent, kept = edges_and_grad(core_id, near, far, *common, dconv_in, turned_rows)
    got = lax.ppermute(sent, "core", swap)
    accept_local = projected(hidden_in, hidden_out, accept_weight, kept)
    chip_half = join(kept, got, accept_local)
    pieces = lax.all_to_all(chip_half, CHIPS, 0, 0, tiled=True)

    accept_other = lax.ppermute(accept_local, "core", swap)
    counts = pair_counts[0]
    hot = (lax.dynamic_index_in_dim(counts, 2 * chip + 1 - core, 0) > slots.shape[2] // 2).astype(jnp.int32)
    donor_table = projected(hidden_in, hidden_out, donor_weight, chip_half)
    donor_emb = donor_rows(donor_pos.reshape(2 * chips, -1), donor_table, chip_half)
    served = serve(core_id, hot, slots, accept_local, accept_other, donor_emb)
    blocks = list(spread(lax.axis_index("z")[None], pieces, lax.axis_size("z")))
    served, blocks[0] = lax.optimization_barrier((served, blocks[0]))
    accepted = lax.all_to_all(served, CHIPS, 0, 0, tiled=True)
    weight_grad = jnp.transpose(dp_sum(blocks, conv_weight.shape[1]), (1, 0, 2))
    junction_pairs = pairs(core[None], counts, donor_emb, accepted)[None]
    return (junction_pairs, weight_grad)


def solution(mesh):
    grid = Mesh(mesh.devices.reshape(8, 2, 2, 4, 2), AXES)
    return jax.shard_map(
        on_device,
        mesh=grid,
        in_specs=(
            P(DP, SEQ, None),
            P(DP, SEQ),
            P(),
            P(),
            P(),
            P(DP, SEQ, None),
            P(DP, SEQ),
            P(DP, SEQ),
            P(DP, SEQ),
            P(),
            P(),
        ),
        out_specs=(P(DP, SEQ, None), P(SEQ, None, DP)),
        check_vma=False,
    )
```

```python
import functools

import jax
import jax.numpy as jnp
from jax import lax
from jax.experimental import pallas as pl
from jax.experimental.pallas import tpu as pltpu
from jax.sharding import Mesh, PartitionSpec as P

DILATION_STEP = 256
AXES = ("z", "yl", "yh", "x", "core")
DP = ("z", "yl")
SEQ = ("yh", "x", "core")
CHIPS = ("yh", "x")
LANES = 128
MIB = 1024 * 1024
TILE = 256
BF16 = jnp.bfloat16
F32 = jnp.float32
GELU_A = 0.7978845608028654
GELU_B = 0.044715


def params(mib):
    return pltpu.CompilerParams(vmem_limit_bytes=mib * MIB)


def cost(flops, nbytes):
    return pl.CostEstimate(flops=flops, bytes_accessed=nbytes, transcendentals=0)


def in_hbm(x):
    return pltpu.with_memory_space_constraint(x, pltpu.HBM)


def dot(a, b):
    return jnp.dot(a, b, preferred_element_type=F32)


def across_lanes(row):
    return jnp.transpose(jnp.broadcast_to(row, (LANES, LANES)))


def summed_inputs(trunk, ids_ref, first, table_ref):
    rows, width = trunk.shape
    parts = []
    for block in range(rows // LANES):
        ids = across_lanes(ids_ref[pl.ds(first + block, 1), :])
        ids = jnp.concatenate([ids] * (width // LANES), axis=1)
        embedded = jnp.where(
            ids < 2,
            jnp.where(ids == 0, table_ref[0:1, :], table_ref[1:2, :]),
            jnp.where(ids == 2, table_ref[2:3, :], table_ref[3:4, :]),
        )
        parts.append(trunk[block * LANES : (block + 1) * LANES].astype(F32) + embedded)
    return jnp.concatenate(parts, axis=0)


def norm_kernel(core_ref, trunk_ref, ids_ref, table_ref, gain_ref, out_ref, near_ref, far_ref):
    i = pl.program_id(0)
    last = pl.num_programs(0) - 1
    per_chunk = trunk_ref.shape[0] // LANES
    inputs = summed_inputs(trunk_ref[...], ids_ref, i * per_chunk, table_ref)
    mean = jnp.mean(inputs * inputs, axis=-1, keepdims=True)
    normed = (inputs * lax.rsqrt(mean + 1e-06) * gain_ref[...][None, :]).astype(BF16)
    out_ref[...] = normed
    chunk = near_ref.shape[0]
    edge = jnp.where(i == 0, normed[:chunk], normed[normed.shape[0] - chunk :])

    @pl.when(i == jnp.where(core_ref[0] == 0, last, 0))
    def _():
        near_ref[...] = edge

    @pl.when(i == jnp.where(core_ref[0] == 0, 0, last))
    def _():
        far_ref[...] = edge


def norm_rows(core, trunk, ids, table, gain):
    length, width = trunk.shape
    chunk = DILATION_STEP
    block = length // 2
    whole = lambda i, c: (0, 0)
    edge = jax.ShapeDtypeStruct((chunk, width), BF16)
    return pl.pallas_call(
        norm_kernel,
        grid_spec=pltpu.PrefetchScalarGridSpec(
            num_scalar_prefetch=1,
            grid=(length // block,),
            in_specs=[
                pl.BlockSpec((block, width), lambda i, c: (i, 0)),
                pl.BlockSpec(ids.shape, whole),
                pl.BlockSpec(table.shape, whole),
                pl.BlockSpec(gain.shape, lambda i, c: (0,)),
            ],
            out_specs=[
                pl.BlockSpec((block, width), lambda i, c: (i, 0)),
                pl.BlockSpec((chunk, width), whole),
                pl.BlockSpec((chunk, width), whole),
            ],
        ),
        out_shape=[jax.ShapeDtypeStruct((length, width), BF16), edge, edge],
        compiler_params=params(60),
        cost_estimate=cost(10 * length * width, 4 * length * width),
    )(core, trunk, ids, table, gain)


def gelu_parts(x):
    square = x * x
    t = jnp.tanh(GELU_A * x * (1.0 + GELU_B * square))
    cdf = 0.5 + 0.5 * t
    slope = cdf + (0.5 * GELU_A) * x * (1.0 - t * t) * (1.0 + (3 * GELU_B) * square)
    return x * cdf, slope


def turned(block, rows):
    width = block.shape[1]
    return jnp.transpose(block).reshape(width // (2 * rows), 2, rows, block.shape[0])


def conv_tile(left, mid, right, chunks, w_ref, trunk_refs, grad_refs, ids_ref, table_ref):
    out = dot(left, w_ref[0]) + dot(mid, w_ref[1]) + dot(right, w_ref[2])
    act, slope = gelu_parts(out)
    chunk = out.shape[0] // 2
    hidden, dconv = [], []
    for part in range(2):
        span = slice(part * chunk, (part + 1) * chunk)
        inputs = summed_inputs(trunk_refs[part][0], ids_ref, 2 * chunks[part], table_ref)
        hidden.append((inputs + act[span]).astype(BF16))
        dconv.append((grad_refs[part][0].astype(F32) * slope[span]).astype(BF16))
    return hidden, dconv


def inner_kernel(n_ref, w_ref, ta_ref, tb_ref, ga_ref, gb_ref, ids_ref, table_ref,
                 hidden_ref, dconv_ref, turned_ref, *, rows):
    chunk = DILATION_STEP
    two = 2 * chunk

    def tile():
        hidden, dconv = conv_tile(
            n_ref[:two], n_ref[chunk : chunk + two], n_ref[two:], (1, 2), w_ref,
            (ta_ref, tb_ref), (ga_ref, gb_ref), ids_ref, table_ref,
        )
        hidden_ref[...] = jnp.concatenate(hidden, axis=0)
        dconv_ref[...] = jnp.concatenate(dconv, axis=0)

    for step in range(2):

        @pl.when(pl.program_id(0) == step)
        def _():
            span = slice(step * two, (step + 1) * two)
            turned_ref[:, :, :, span] = turned(n_ref[span], rows)
            tile()

    pl.when(pl.program_id(0) == 2)(tile)


def conv_inner(normed, weight, trunk, grad, ids, table, rows):
    length, width = normed.shape
    chunk = DILATION_STEP
    groups = width // (2 * rows)
    whole = lambda n: (0, 0)
    part = lambda c: pl.BlockSpec((1, chunk, TILE), lambda n: (c, 0, n))
    out = pl.BlockSpec((2 * chunk, TILE), lambda n: (0, n))
    half = jax.ShapeDtypeStruct((2 * chunk, width), BF16)
    turned_shape = (groups, 2, rows, length)
    return pl.pallas_call(
        functools.partial(inner_kernel, rows=rows),
        grid=(width // TILE,),
        in_specs=[
            pl.BlockSpec(normed.shape, whole),
            pl.BlockSpec((3, width, TILE), lambda n: (0, 0, n)),
            part(1), part(2), part(1), part(2),
            pl.BlockSpec(ids.shape, whole),
            pl.BlockSpec((table.shape[0], TILE), lambda n: (0, n)),
        ],
        out_specs=[out, out, pl.BlockSpec(turned_shape, lambda n: (0, 0, 0, 0))],
        out_shape=[half, half, jax.ShapeDtypeStruct(turned_shape, BF16)],
        compiler_params=params(60),
        cost_estimate=cost(3 * length * width * width, 8 * length * width),
    )(normed, weight, trunk, trunk, grad, grad, ids, table)


def edge_kernel(core_ref, near_ref, far_ref, n_ref, w_ref, ta_ref, tb_ref, ga_ref, gb_ref, ids_ref, table_ref,
                inner_ref, turned_ref, hidden_ref, sent_ref, kept_ref, dconv_ref, window_ref, sems, *, rows):
    step = pl.program_id(0)
    chunk = near_ref.shape[0]
    length, width = n_ref.shape
    tiles = width // TILE
    first = core_ref[0] == 0
    part = lambda i: n_ref[i * chunk : (i + 1) * chunk]
    fetches = [
        pltpu.make_async_copy(inner_ref, dconv_ref.at[chunk : 3 * chunk], sems.at[0]),
        pltpu.make_async_copy(turned_ref, window_ref.at[:, :, :, chunk : chunk + length], sems.at[1]),
    ]

    @pl.when(step == 0)
    def _():
        for fetch in fetches:
            fetch.start()

    def conv(tile):
        low = jnp.where(first, far_ref[...], near_ref[...])
        high = jnp.where(first, near_ref[...], far_ref[...])
        left = jnp.concatenate([low, part(2)], axis=0)
        mid = jnp.concatenate([part(0), part(3)], axis=0)
        right = jnp.concatenate([part(1), high], axis=0)
        hidden, dconv = conv_tile(left, mid, right, (0, 3), w_ref, (ta_ref, tb_ref), (ga_ref, gb_ref),
                                  ids_ref, table_ref)
        hidden_ref[...] = jnp.concatenate(hidden, axis=0)
        span = slice(tile * TILE, (tile + 1) * TILE)
        dconv_ref[:chunk, span] = dconv[0]
        dconv_ref[3 * chunk :, span] = dconv[1]
        if tile == 0:
            window_ref[:, :, :, :chunk] = turned(low, rows)
        if tile == 1:
            window_ref[:, :, :, chunk + length :] = turned(high, rows)

    for tile in range(tiles):
        pl.when(step == tile)(functools.partial(conv, tile))

    for tap in range(3):

        @pl.when(step == tiles + tap)
        def _():
            if tap == 0:
                for fetch in fetches:
                    fetch.wait()
            window = window_ref[:, :, :, tap * chunk : tap * chunk + length]
            value = dot(window.reshape(width, length), dconv_ref[...])
            value = value.reshape(width // (2 * rows), 2, rows, width)
            kept_ref[:, 0] = jnp.where(first, value[:, 0], value[:, 1]).astype(BF16)
            sent_ref[:, 0] = jnp.where(first, value[:, 1], value[:, 0]).astype(BF16)


def edges_and_grad(core, near, far, normed, weight, trunk, grad, ids, table, inner, turned_rows):
    length, width = normed.shape
    chunk = near.shape[0]
    groups, _, rows, _ = turned_rows.shape
    tiles, taps = width // TILE, weight.shape[0]
    whole = lambda n, c: (0, 0)
    tile = lambda n: jnp.minimum(n, tiles - 1)
    part = lambda k: pl.BlockSpec((1, chunk, TILE), lambda n, c: (k, 0, tile(n)))
    block = pl.BlockSpec((groups, 1, rows, width), lambda n, c: (0, jnp.maximum(n - tiles, 0), 0, 0))
    piece = jax.ShapeDtypeStruct((groups, taps, rows, width), BF16)
    return pl.pallas_call(
        functools.partial(edge_kernel, rows=rows),
        grid_spec=pltpu.PrefetchScalarGridSpec(
            num_scalar_prefetch=1,
            grid=(tiles + taps,),
            in_specs=[
                pl.BlockSpec(near.shape, whole),
                pl.BlockSpec(far.shape, whole),
                pl.BlockSpec(normed.shape, whole),
                pl.BlockSpec((taps, width, TILE), lambda n, c: (0, 0, tile(n))),
                part(0), part(3), part(0), part(3),
                pl.BlockSpec(ids.shape, whole),
                pl.BlockSpec((table.shape[0], TILE), lambda n, c: (0, tile(n))),
                pl.BlockSpec(memory_space=pl.ANY),
                pl.BlockSpec(memory_space=pl.ANY),
            ],
            out_specs=[pl.BlockSpec((2 * chunk, TILE), lambda n, c: (0, tile(n))), block, block],
            scratch_shapes=[
                pltpu.VMEM((length, width), BF16),
                pltpu.VMEM((groups, 2, rows, length + 2 * chunk), BF16),
                pltpu.SemaphoreType.DMA((2,)),
            ],
        ),
        out_shape=[
            pltpu.HBM((2 * chunk, width), BF16),
            pltpu.HBM(piece.shape, BF16),
            piece,
        ],
        compiler_params=params(34),
        cost_estimate=cost(9 * length * width * width, 20 * length * width),
    )(core, near, far, *[in_hbm(v) for v in (normed, weight, trunk, trunk, grad, grad, ids, table, inner, turned_rows)])


def table_kernel(inner_ref, outer_ref, weight_ref, after_ref, out_ref):
    del after_ref
    half = inner_ref.shape[0]
    out_ref[:half] = dot(inner_ref[...], weight_ref[...]).astype(BF16)
    out_ref[half:] = dot(outer_ref[...], weight_ref[...]).astype(BF16)


def projected(inner, outer, weight, after):
    half, width = inner.shape
    whole = lambda n: (0, 0)
    tile = lambda count: pl.BlockSpec((count, TILE), lambda n: (0, n))
    return pl.pallas_call(
        table_kernel,
        grid=(width // TILE,),
        in_specs=[
            pl.BlockSpec(inner.shape, whole),
            pl.BlockSpec(outer.shape, whole),
            tile(width),
            pl.BlockSpec(memory_space=pl.ANY),
        ],
        out_specs=tile(2 * half),
        out_shape=pltpu.HBM((2 * half, width), BF16),
        compiler_params=params(12),
        cost_estimate=cost(4 * half * width * width, 8 * half * width),
    )(in_hbm(inner), in_hbm(outer), in_hbm(weight), after)


def table_place(position):
    chunk = DILATION_STEP
    moved = jnp.where(position < 3 * chunk, position - chunk, position)
    return jnp.where(position < chunk, position + 2 * chunk, moved)


def join_kernel(kept_ref, got_ref, after_ref, out_ref):
    del after_ref
    out_ref[...] = (kept_ref[...].astype(F32) + got_ref[...].astype(F32)).astype(BF16)


def join(kept, got, after):
    groups, taps, rows, width = kept.shape
    block = pl.BlockSpec((groups // 2, taps, rows, width), lambda i: (i, 0, 0, 0))
    return pl.pallas_call(
        join_kernel,
        grid=(2,),
        in_specs=[block, block, pl.BlockSpec(memory_space=pl.ANY)],
        out_specs=block,
        out_shape=pltpu.HBM(kept.shape, BF16),
        compiler_params=params(12),
        cost_estimate=cost(kept.size, 6 * kept.size),
    )(kept, got, in_hbm(after))


def selected(index_rows, table_ref):
    lane = lax.broadcasted_iota(jnp.int32, (LANES, LANES), 1)
    picks = []
    for row in index_rows:
        index = across_lanes(table_place(row))
        picks.append(
            jnp.concatenate(
                [
                    jnp.where(index == lane + b * LANES, 1.0, 0.0).astype(BF16)
                    for b in range(table_ref.shape[0] // LANES)
                ],
                axis=1,
            )
        )
    return dot(jnp.concatenate(picks, axis=0), table_ref[...]).astype(BF16)


def serve_kernel(core_ref, hot_ref, index_ref, own_ref, other_ref, after_ref, out_ref):
    del after_ref
    half = LANES // 2
    per = out_ref.shape[0]
    core = core_ref[0]
    asked = lambda k: [index_ref[pl.program_id(0) * per + q, pl.ds(k, 1), :] for q in range(per)]
    own = selected(asked(core), own_ref)
    other = selected(asked(1 - core), other_ref)
    hot = hot_ref[0] != 0
    for q in range(per):
        low, high = q * LANES, q * LANES + half
        out_ref[q, 0] = own[low:high]
        out_ref[q, 1] = other[low:high]

    @pl.when(jnp.logical_not(hot))
    def _():
        for q in range(per):
            out_ref[q, 2] = own[q * LANES + half : (q + 1) * LANES]

    @pl.when(hot)
    def _():
        for q in range(per):
            out_ref[q, 2] = other[q * LANES + half : (q + 1) * LANES]


def serve(core, hot, index, own, other, after):
    groups = index.shape[0]
    width = own.shape[1]
    per = 4
    whole = lambda q, c, h: (0, 0)
    return pl.pallas_call(
        serve_kernel,
        grid_spec=pltpu.PrefetchScalarGridSpec(
            num_scalar_prefetch=2,
            grid=(groups // per,),
            in_specs=[
                pl.BlockSpec(index.shape, lambda q, c, h: (0, 0, 0)),
                pl.BlockSpec(own.shape, whole),
                pl.BlockSpec(other.shape, whole),
                pl.BlockSpec(memory_space=pl.ANY),
            ],
            out_specs=pl.BlockSpec((per, 3, LANES // 2, width), lambda q, c, h: (q, 0, 0, 0)),
        ),
        out_shape=jax.ShapeDtypeStruct((groups, 3, LANES // 2, width), BF16),
        compiler_params=params(60),
        cost_estimate=cost(4 * groups * LANES * own.shape[0] * width, 8 * own.size),
    )(core, hot, index, own, other, in_hbm(after))


def donor_kernel(index_ref, table_ref, after_ref, out_ref):
    del after_ref
    per = out_ref.shape[0] // LANES
    first = pl.program_id(0) * per
    out_ref[...] = selected([index_ref[pl.ds(first + r, 1), :] for r in range(per)], table_ref)


def donor_rows(index, table, after):
    count = index.shape[0]
    width = table.shape[1]
    per = 4
    whole = lambda q: (0, 0)
    return pl.pallas_call(
        donor_kernel,
        grid=(count // per,),
        in_specs=[
            pl.BlockSpec(index.shape, whole),
            pl.BlockSpec(table.shape, whole),
            pl.BlockSpec(memory_space=pl.ANY),
        ],
        out_specs=pl.BlockSpec((per * LANES, width), lambda q: (q, 0)),
        out_shape=jax.ShapeDtypeStruct((count * LANES, width), BF16),
        compiler_params=params(60),
        cost_estimate=cost(2 * count * LANES * table.shape[0] * width, 10 * table.size),
    )(index, table, in_hbm(after))


def pair_kernel(core_ref, counts_ref, donor_ref, accepted_ref, out_ref):
    half = LANES // 2
    per = accepted_ref.shape[0]
    slot = lax.broadcasted_iota(jnp.int32, (half, LANES), 0)
    copies = out_ref.shape[1] // LANES
    for q in range(per):
        group = pl.program_id(0) * per + q
        for owner_core in range(2):
            count = counts_ref[2 * group + owner_core]
            place = lax.rem(core_ref[0] + owner_core, 2)
            for part, source in enumerate((place, 2)):
                at = (2 * q + owner_core) * LANES + part * half
                mask = jnp.where(slot + part * half < count, 1.0, 0.0).astype(BF16)
                mask = jnp.concatenate([mask] * copies, axis=1)
                out_ref[at : at + half] = accepted_ref[q, source] * donor_ref[at : at + half] * mask


def pairs(core, counts, donor, accepted):
    groups = accepted.shape[0]
    width = donor.shape[1]
    per = 4
    rows = pl.BlockSpec((2 * per * LANES, width), lambda q, c, n: (q, 0))
    return pl.pallas_call(
        pair_kernel,
        grid_spec=pltpu.PrefetchScalarGridSpec(
            num_scalar_prefetch=2,
            grid=(groups // per,),
            in_specs=[rows, pl.BlockSpec((per,) + accepted.shape[1:], lambda q, c, n: (q, 0, 0, 0))],
            out_specs=rows,
        ),
        out_shape=jax.ShapeDtypeStruct(donor.shape, BF16),
        compiler_params=params(16),
        cost_estimate=cost(2 * donor.size, 6 * donor.size),
    )(core, counts, in_hbm(donor), accepted)


def spread_kernel(z_ref, pieces_ref, *refs):
    outs, scratch = refs[:-1], refs[-1]
    chips, taps, rows, width = pieces_ref.shape
    total = pieces_ref[0].astype(F32)
    for i in range(1, chips):
        total = total + pieces_ref[i].astype(F32)
    scratch[...] = jnp.transpose(total.reshape(taps * rows, width))
    count = len(outs)
    size = width // count
    for step, out in enumerate(outs):
        start = pl.multiple_of(lax.rem(z_ref[0] + step, count) * size, size)
        out[...] = scratch[pl.ds(start, size), :].astype(out.dtype)


def spread(z, pieces, count):
    chips, taps, rows, width = pieces.shape
    shape = (width // count, taps * rows)
    return pl.pallas_call(
        spread_kernel,
        grid_spec=pltpu.PrefetchScalarGridSpec(
            num_scalar_prefetch=1,
            grid=(1,),
            in_specs=[pl.BlockSpec(pieces.shape, lambda i, z: (0, 0, 0, 0))],
            out_specs=[pl.BlockSpec(shape, lambda i, z: (0, 0))] * count,
            scratch_shapes=[pltpu.VMEM((width, taps * rows), F32)],
        ),
        out_shape=[pltpu.HBM(shape, BF16 if k else F32) for k in range(count)],
        compiler_params=params(12),
        cost_estimate=cost(2 * pieces.size, 3 * pieces.size),
    )(z, pieces)


def gather_kernel(yl_ref, own_ref, *refs):
    got, (kept_ref, sent_ref) = refs[:-2], refs[-2:]
    half = kept_ref.shape[0]

    def total(start):
        value = own_ref[start : start + half]
        for ref in got:
            value = value + ref[start : start + half].astype(F32)
        return value

    for yl in range(2):

        @pl.when(yl_ref[0] == yl)
        def _():
            kept_ref[...] = total(yl * half)
            sent_ref[...] = total((1 - yl) * half).astype(BF16)


def gathered(yl, own, got):
    rows, width = own.shape
    whole = lambda i, y: (0, 0)
    full = pl.BlockSpec(own.shape, whole)
    half = pl.BlockSpec((rows // 2, width), whole)
    return pl.pallas_call(
        gather_kernel,
        grid_spec=pltpu.PrefetchScalarGridSpec(
            num_scalar_prefetch=1, grid=(1,), in_specs=[full] * (1 + len(got)), out_specs=[half, half]
        ),
        out_shape=[
            jax.ShapeDtypeStruct((rows // 2, width), F32),
            jax.ShapeDtypeStruct((rows // 2, width), BF16),
        ],
        compiler_params=params(8),
        cost_estimate=cost(8 * own.size, 20 * own.size),
    )(yl, own, *got)


def final_kernel(kept_ref, got_ref, out_ref):
    total = kept_ref[...] + got_ref[...].astype(F32)
    out_ref[...] = jnp.transpose(total).reshape(out_ref.shape)


def final_grad(kept, got, taps):
    cols, width = kept.shape
    return pl.pallas_call(
        final_kernel,
        out_shape=jax.ShapeDtypeStruct((taps, width // taps, cols), F32),
        compiler_params=params(8),
    )(kept, got)


def dp_sum(outs, taps):
    nz = len(outs)
    got = [
        lax.ppermute(outs[step], "z", [(i, (i + step) % nz) for i in range(nz)])
        for step in range(1, nz)
    ]
    kept, sent = gathered(lax.axis_index("yl")[None], outs[0], got)
    return final_grad(kept, lax.ppermute(sent, "yl", [(0, 1), (1, 0)]), taps)


def on_device(
    trunk_acts,
    base_ids,
    base_table,
    norm_gain,
    conv_weight,
    grad_out,
    donor_pos,
    accept_pos,
    pair_counts,
    donor_weight,
    accept_weight,
):
    core = lax.axis_index("core")
    chip = lax.axis_index(CHIPS)
    trunk = trunk_acts[0]
    length, width = trunk.shape
    seq_count = lax.axis_size(SEQ)
    rows = width // seq_count
    chips = seq_count // 2
    ids = base_ids.reshape(length // LANES, LANES)
    weight = jnp.transpose(conv_weight, (1, 0, 2))
    swap = [(0, 1), (1, 0)]
    split = lambda v: v.reshape(length // DILATION_STEP, DILATION_STEP, width)
    core_id = core[None]

    slots = lax.all_to_all(accept_pos.reshape(chips, 2, -1), CHIPS, 0, 0, tiled=True)
    normed, near, far = norm_rows(core_id, trunk, ids, base_table, norm_gain)
    borders = [(i, i + 1) for i in range(1, seq_count - 1, 2)]
    far = lax.ppermute(far, SEQ, borders + [(target, source) for source, target in borders])
    slots, near = lax.optimization_barrier((slots, near))
    near = lax.ppermute(near, "core", swap)
    common = (normed, weight, split(trunk_acts), split(grad_out), ids, base_table)
    hidden_in, dconv_in, turned_rows = conv_inner(*common, rows)
    hidden_out, sent, kept = edges_and_grad(core_id, near, far, *common, dconv_in, turned_rows)
    got = lax.ppermute(sent, "core", swap)
    accept_local = projected(hidden_in, hidden_out, accept_weight, kept)
    chip_half = join(kept, got, accept_local)
    pieces = lax.all_to_all(chip_half, CHIPS, 0, 0, tiled=True)

    accept_other = lax.ppermute(accept_local, "core", swap)
    counts = pair_counts[0]
    hot = (lax.dynamic_index_in_dim(counts, 2 * chip + 1 - core, 0) > slots.shape[2] // 2).astype(jnp.int32)
    donor_table = projected(hidden_in, hidden_out, donor_weight, chip_half)
    donor_emb = donor_rows(donor_pos.reshape(2 * chips, -1), donor_table, chip_half)
    served = serve(core_id, hot, slots, accept_local, accept_other, donor_emb)
    blocks = list(spread(lax.axis_index("z")[None], pieces, lax.axis_size("z")))
    served, blocks[0] = lax.optimization_barrier((served, blocks[0]))
    accepted = lax.all_to_all(served, CHIPS, 0, 0, tiled=True)
    weight_grad = jnp.transpose(dp_sum(blocks, conv_weight.shape[1]), (1, 0, 2))
    junction_pairs = pairs(core[None], counts, donor_emb, accepted)[None]
    return (junction_pairs, weight_grad)


def solution(mesh):
    grid = Mesh(mesh.devices.reshape(8, 2, 2, 4, 2), AXES)
    return jax.shard_map(
        on_device,
        mesh=grid,
        in_specs=(
            P(DP, SEQ, None),
            P(DP, SEQ),
            P(),
            P(),
            P(),
            P(DP, SEQ, None),
            P(DP, SEQ),
            P(DP, SEQ),
            P(DP, SEQ),
            P(),
            P(),
        ),
        out_specs=(P(DP, SEQ, None), P(SEQ, None, DP)),
        check_vma=False,
    )
```
